256 devices in a mesh: box: 32 (over y, x, core), term: 8 (over z).
Axes of the slice: x: 4, y: 4, z: 8, core: 2. Of those that a mesh axis runs over, the one named last changes fastest.
Arguments:
- coeffs: bfloat16 [16, 512, 256], P(None, 'box'), may hold values from -6 to 6
- operators: bfloat16 [16, 3, 16, 16], P('term'), may hold values from -1.5 to 1.5
- neighbors: int32 [512, 13], P('box'), may hold values from -1 to 511, as said below
Outputs:
- potential: float32 [16, 512, 256], P('term', 'box')
The draws below stay inside these ranges and needn't reach their ends.
Inputs may be any that keep to these rules, and one draw needn't show every extreme that they name: `neighbors`: entry (b, k) is the index of the box at displacement k from box b, or -1 where that box is not in the level; it is never b. Among the 16 rows of one index of box, at most 2 entries name boxes of any one other index (boxes 16 * q to 16 * q + 15); each index has exactly 2 entries naming boxes of each index next to it, and one index receives exactly 2 such entries from every other index.
All inputs are finite; a program needn't handle non-finite values.
Results may differ from the reference program's by a relative error of at most 0.0018.
Values may be sent and summed in bfloat16 or wider, within the bound.
No kernel may reach another device: no remote copies, remote signals or barrier semaphores. Data moves between devices by JAX's collectives and lax.ppermute only.
A program may use at most 128 MiB of HBM per device.

```python
import math
import jax
import jax.numpy as jnp
from jax import lax

K = 16
R = 16
BOX_DEV = 16
CAP = 2
BOXES = 512


def draw_operators(key, part):
    subkeys = jax.random.split(key, 5)
    weight_scale = jnp.exp(jax.random.uniform(subkeys[0], (R, 1, 1), jnp.float32, math.log(0.25), math.log(0.7)))
    noise = jnp.clip(jax.random.normal(subkeys[1], (R, K, K), jnp.float32), -4.0, 4.0)
    far_noise = jnp.clip(jax.random.normal(subkeys[2], (R, K, K), jnp.float32), -4.0, 4.0)
    diag_near = jax.random.uniform(subkeys[3], (R, K), jnp.float32, 0.6, 1.4)
    diag_far = jax.random.uniform(subkeys[4], (R, K), jnp.float32, 0.3, 1.0)
    identity = jnp.eye(K, dtype=jnp.float32)
    center = weight_scale * (identity * diag_near[:, None, :] + 0.4 * (noise + jnp.transpose(noise, (0, 2, 1))) / math.sqrt(2.0 * K))
    ahead = weight_scale * 0.7 * (identity * diag_far[:, None, :] + 0.5 * far_noise / math.sqrt(1.0 * K))
    behind = jnp.transpose(ahead, (0, 2, 1))
    return jnp.stack([behind, center, ahead], axis=1).astype(jnp.bfloat16)


def draw_neighbors(key, part):
    groups = BOXES // BOX_DEV
    entries = BOX_DEV * 13
    subkeys = jax.random.split(key, 7)
    hub_device = jax.random.randint(subkeys[0], (), 0, groups)
    sender = jnp.arange(groups)[:, None]
    receiver = jnp.arange(groups)[None, :]
    loose = jax.random.randint(subkeys[1], (groups, groups), 0, CAP + 1)
    filled = (jnp.abs(sender - receiver) == 1) | (receiver == hub_device)
    counts = jnp.where(sender == receiver, 0, jnp.where(filled, CAP, loose))
    slot_peer = jnp.repeat(jnp.arange(groups), CAP)
    slot_rank = jnp.tile(jnp.arange(CAP), groups)
    usable = slot_rank[None, :] < counts[:, slot_peer]
    chosen = jax.random.randint(subkeys[2], (groups, groups * CAP), 0, BOX_DEV)
    remote_target = slot_peer[None, :] * BOX_DEV + chosen
    padding = entries - groups * CAP
    usable_all = jnp.concatenate([usable, jnp.zeros((groups, padding), bool)], axis=1)
    target_all = jnp.concatenate([remote_target, jnp.zeros((groups, padding), jnp.int32)], axis=1)
    placing = jax.vmap(lambda sub: jax.random.permutation(sub, entries))(jax.random.split(subkeys[3], groups))
    position = jnp.argsort(placing, axis=1)
    is_remote = jnp.take_along_axis(usable_all, position, axis=1)
    remote_box = jnp.take_along_axis(target_all, position, axis=1)
    density = jax.random.randint(subkeys[4], (groups, 1), 1, 5)
    fill_roll = jax.random.randint(subkeys[5], (groups, entries), 0, 4)
    absent = fill_roll >= density
    own_box = jnp.arange(entries)[None, :] // 13
    offset = jax.random.randint(subkeys[6], (groups, entries), 1, BOX_DEV)
    local_box = sender * BOX_DEV + (own_box + offset) % BOX_DEV
    result = jnp.where(is_remote, remote_box, jnp.where(absent, -1, local_box))
    return result.reshape(BOXES, 13).astype(jnp.int32)


def level_of(key, dims, shards, low, top_value):
    gain = 1.0
    for axis_at, parts in shards:
        heights = jax.random.uniform(jax.random.fold_in(jax.random.fold_in(key, 6), axis_at), (parts,), jnp.float32, low / len(shards), top_value / len(shards))
        gain = gain * jnp.repeat(jnp.exp(heights), dims[axis_at] // parts).reshape((-1,) + (1,) * (len(dims) - 1 - axis_at))
    return gain


def scatter_about(key, shape, width, limit, shards=(), kind=jnp.bfloat16):
    values = width * jax.random.normal(key, shape, jnp.float32)
    if shards:
        values = values * level_of(key, shape, shards, -0.22, 0.18)
    return jnp.clip(values, -limit, limit).astype(kind)


def setup_inputs(seed: int = 0) -> dict:
    key_list = jax.random.split(jax.random.key(seed), 4)
    coeffs = scatter_about(key_list[0], (K, BOXES, K * K), 1.0, 6.0, ((1, 32),))
    operators = draw_operators(jax.random.fold_in(key_list[3], 71), 0)
    neighbors = draw_neighbors(jax.random.fold_in(key_list[3], 71), 0)
    return {"coeffs": coeffs, "operators": operators, "neighbors": neighbors}


def through_bf16(values):
    return lax.optimization_barrier(values.astype(jnp.bfloat16)).astype(jnp.float32)


def add_code(result, applied, position, targets, present):
    if position == 13:
        return result + applied
    if position > 13:
        column = position - 14
        picked = jnp.take(applied, targets[:, column], axis=1)
        return result + jnp.where(present[:, column][None, :, None], picked, 0.0)
    column = 12 - position
    masked = jnp.where(present[:, column][None, :, None], applied, 0.0)
    return result.at[:, targets[:, column], :].add(masked)


def reference(coeffs, operators, neighbors):
    degree = coeffs.shape[0]
    box_count = coeffs.shape[1]
    plane_size = coeffs.shape[2]
    term_count = operators.shape[0]
    source = coeffs.astype(jnp.float32)
    blocks_all = operators.astype(jnp.float32)
    present = neighbors >= 0
    targets = jnp.where(present, neighbors, 0).astype(jnp.int32)
    result = jnp.zeros((degree, box_count, plane_size), jnp.float32)
    for x_block in range(3):
        x_applied = jnp.einsum('rac,cbv->rabv', blocks_all[:, x_block], source, precision=lax.Precision.HIGHEST)
        x_applied = through_bf16(x_applied)
        for y_block in range(3):
            for z_block in range(3):
                kronecker = jnp.einsum('rac,rbd->rabcd', blocks_all[:, y_block], blocks_all[:, z_block], precision=lax.Precision.HIGHEST)
                kronecker = through_bf16(kronecker.reshape(term_count, plane_size, plane_size))
                applied = jnp.einsum('rabv,ruv->abu', x_applied, kronecker, precision=lax.Precision.HIGHEST)
                position = 9 * x_block + 3 * y_block + z_block
                result = add_code(result, applied, position, targets, present)
    return result
```

```python
import jax
import jax.numpy as jnp
from jax import lax
from jax.experimental import pallas as pl
from jax.experimental.pallas import tpu as pltpu
from jax.sharding import PartitionSpec as P

CAP = 2
BIG = 0x7FFFFFFF


def iota(shape, axis):
    return lax.broadcasted_iota(jnp.int32, shape, axis)


def request_kernel(place_ref, neighbors_ref, keys_ref):
    box_count, column_count = neighbors_ref.shape
    groups = keys_ref.shape[0]
    myself = place_ref[0]
    peer = iota((groups, column_count), 0)
    column = iota((groups, column_count), 1)
    first = jnp.full((groups, column_count), BIG, jnp.int32)
    last = jnp.full((groups, column_count), -1, jnp.int32)
    for home in range(box_count):
        named = neighbors_ref[home : home + 1, :]
        owner = jnp.where(named >= 0, named >> 4, -1)
        owner = jnp.where(owner == myself, -1, owner)
        key = ((home * column_count + column) << 16) | (column << 8) | (home << 4) | (named & 15)
        member = jnp.broadcast_to(owner, peer.shape) == peer
        first = jnp.minimum(first, jnp.where(member, key, BIG))
        last = jnp.maximum(last, jnp.where(member, key, -1))
    first = jnp.min(first, axis=1, keepdims=True)
    last = jnp.max(last, axis=1, keepdims=True)
    last = jnp.where(last == first, -1, last)
    first = jnp.where(first == BIG, -1, first)
    lane = iota(keys_ref.shape, 1)
    keys_ref[...] = jnp.where(lane == 0, first, jnp.where(lane == 1, last, -1))


def expand(rows, modulo):
    lane = iota((16, 256), 1)
    row = iota((16, 256), 0)
    pick = (lane & 15) if modulo else (lane >> 4)
    ones = jnp.where(pick == row, 1.0, 0.0).astype(jnp.bfloat16)
    return jnp.dot(rows, ones, preferred_element_type=jnp.float32)


def image_kernel(
    place_ref, keys_ref, guests_ref, neighbors_ref, coeffs_ref, *rest
):
    pieces, (local_ref, message_ref, outer_ref, inner_ref, left_ref, half_ref, kron_ref, image_ref) = (
        rest[:8],
        rest[8:],
    )
    myself = place_ref[0]
    term = place_ref[1]
    rows = jnp.concatenate([piece[...] for piece in pieces], axis=0)
    outer_ref[...] = expand(rows, False)
    inner_ref[...] = expand(rows, True)
    diagonal = (iota((16, 256), 1) & 15) == iota((16, 256), 0)
    for r in range(16):
        for m in range(3):
            for al in range(2):
                row = outer_ref[pl.ds((3 * r + m) * 16 + 2 * term + al, 1), :]
                block = jnp.where(diagonal, jnp.broadcast_to(row, (16, 256)), 0.0)
                at = 96 * r + 32 * m + 16 * al
                left_ref[at : at + 16, :] = block.astype(jnp.bfloat16)
    half = jnp.dot(left_ref[...], coeffs_ref[...], preferred_element_type=jnp.float32)
    half = half.astype(jnp.bfloat16)
    for r in range(16):
        half_ref[:, 256 * r : 256 * (r + 1)] = half[96 * r : 96 * (r + 1), :]
    for n in range(3):
        for p in range(3):
            slot = (3 * n + p) % 2
            for r in range(16):
                outer = outer_ref[(3 * r + n) * 16 : (3 * r + n + 1) * 16, :]
                inner = inner_ref[(3 * r + p) * 16 : (3 * r + p + 1) * 16, :]
                product = outer[:, None, :] * inner[None, :, :]
                kron_ref[slot, :, 256 * r : 256 * (r + 1)] = product.reshape(256, 256).astype(
                    jnp.bfloat16
                )
            applied = lax.dot_general(
                half_ref[...],
                kron_ref[slot],
                (((1,), (1,)), ((), ())),
                preferred_element_type=jnp.float32,
            )
            for m in range(3):
                code = 9 * m + 3 * n + p
                for al in range(2):
                    at = 32 * m + 16 * al
                    image_ref[16 * code : 16 * (code + 1), 256 * al : 256 * (al + 1)] = applied[
                        at : at + 16, :
                    ]
    image = image_ref[...]
    high = image.astype(jnp.bfloat16)
    low = (image - high.astype(jnp.float32)).astype(jnp.bfloat16)
    named = neighbors_ref[...]
    within = named - 16 * myself
    within = jnp.where((within >= 0) & (within < 16), within, -1).astype(jnp.float32)
    within = within.astype(jnp.bfloat16)
    lane = iota((13, 208), 1)
    row = iota((13, 208), 0)
    ahead = jnp.where((lane >> 4) == row, 1.0, 0.0).astype(jnp.bfloat16)
    behind = jnp.where((lane >> 4) == 12 - row, 1.0, 0.0).astype(jnp.bfloat16)
    pull = jnp.dot(within, ahead, preferred_element_type=jnp.float32).astype(jnp.int32)
    push = jnp.dot(within, behind, preferred_element_type=jnp.float32)
    lane = iota((16, 208), 1) & 15
    row = iota((16, 208), 0)
    push = jnp.sum(jnp.where(lane == row, push, 0.0), axis=0, keepdims=True).astype(jnp.int32)
    pull_mask = jnp.where(pull == lane, 1.0, 0.0)
    push_mask = jnp.where(jnp.broadcast_to(push, row.shape) == row, 1.0, 0.0)
    same_mask = jnp.where(iota((16, 16), 0) == iota((16, 16), 1), 1.0, 0.0)
    mask = jnp.concatenate([push_mask, same_mask, pull_mask], axis=1).astype(jnp.bfloat16)
    local_ref[...] = jnp.dot(mask, high, preferred_element_type=jnp.float32) + jnp.dot(
        mask, low, preferred_element_type=jnp.float32
    )
    spots = []
    for slot in range(CAP):
        key = keys_ref[:, slot : slot + 1]
        spot = (12 - ((key >> 8) & 15)) * 16 + ((key >> 4) & 15)
        spots.append(jnp.where(key < 0, -1, spot))
    for slot in range(CAP):
        key = guests_ref[:, slot : slot + 1]
        spot = (14 + ((key >> 8) & 15)) * 16 + (key & 15)
        spots.append(jnp.where(key < 0, -1, spot))
    lane = iota((32, 432), 1)
    picks = jnp.concatenate(
        [jnp.where(lane == spot, 1.0, 0.0).astype(jnp.bfloat16) for spot in spots], axis=0
    )
    picked = jnp.dot(picks, high, preferred_element_type=jnp.float32).astype(jnp.bfloat16)
    for slot in range(2 * CAP):
        message_ref[:, 512 * slot : 512 * (slot + 1)] = picked[32 * slot : 32 * (slot + 1), :]


def gather_kernel(keys_ref, guests_ref, local_ref, arrived_ref, out_ref):
    lane = iota((32, 16), 1)
    total = local_ref[...]
    for slot in range(2 * CAP):
        if slot < CAP:
            key = guests_ref[:, slot : slot + 1]
            target = jnp.where(key < 0, -1, key & 15)
        else:
            key = keys_ref[:, slot - CAP : slot - CAP + 1]
            target = jnp.where(key < 0, -1, (key >> 4) & 15)
        pick = jnp.where(lane == target, 1.0, 0.0).astype(jnp.bfloat16)
        total = total + lax.dot_general(
            pick,
            arrived_ref[:, 512 * slot : 512 * (slot + 1)],
            (((0,), (0,)), ((), ())),
            preferred_element_type=jnp.float32,
        )
    for al in range(2):
        out_ref[al] = total[:, 256 * al : 256 * (al + 1)]


def on_device(coeffs, operators, neighbors):
    degree, box_count, plane_size = coeffs.shape
    groups = lax.axis_size("box")
    terms = lax.axis_size("term")
    myself = lax.axis_index("box").astype(jnp.int32)
    term = lax.axis_index("term").astype(jnp.int32)
    place = jnp.stack([myself, term])
    vmem = pl.BlockSpec(memory_space=pltpu.VMEM)
    smem = pl.BlockSpec(memory_space=pltpu.SMEM)
    mine = operators.reshape(-1, degree)
    pieces = [mine]
    for shift in range(1, terms):
        pieces.append(
            lax.ppermute(mine, "term", [(i, (i + shift) % terms) for i in range(terms)])
        )
    keys = pl.pallas_call(
        request_kernel,
        out_shape=jax.ShapeDtypeStruct((groups, 128), jnp.int32),
        in_specs=[smem, vmem],
        out_specs=vmem,
        name="request",
    )(place, neighbors)
    guests = lax.all_to_all(keys, "box", split_axis=0, concat_axis=0, tiled=True)
    local, message = pl.pallas_call(
        image_kernel,
        out_shape=(
            jax.ShapeDtypeStruct((box_count, 2 * plane_size), jnp.float32),
            jax.ShapeDtypeStruct((groups, 4 * CAP * plane_size), jnp.bfloat16),
        ),
        in_specs=[smem] + [vmem] * (4 + terms),
        out_specs=(vmem, vmem),
        scratch_shapes=[
            pltpu.VMEM((768, 256), jnp.float32),
            pltpu.VMEM((768, 256), jnp.float32),
            pltpu.VMEM((1536, 256), jnp.bfloat16),
            pltpu.VMEM((96, 4096), jnp.bfloat16),
            pltpu.VMEM((2, 256, 4096), jnp.bfloat16),
            pltpu.VMEM((432, 512), jnp.float32),
        ],
        name="image",
    )(place, keys, guests, neighbors, coeffs.reshape(degree * box_count, plane_size), *pieces)
    arrived = lax.all_to_all(message, "box", split_axis=0, concat_axis=0, tiled=True)
    return pl.pallas_call(
        gather_kernel,
        out_shape=jax.ShapeDtypeStruct((2, box_count, plane_size), jnp.float32),
        in_specs=[vmem] * 4,
        out_specs=vmem,
        name="gather",
    )(keys, guests, local, arrived)


def solution(mesh):
    placed = (P(None, "box", None), P("term", None, None, None), P("box", None))
    return jax.shard_map(
        on_device, mesh=mesh, in_specs=placed, out_specs=P("term", "box", None), check_vma=False
    )
```

```python
import jax
import jax.numpy as jnp
from jax import lax
from jax.experimental import pallas as pl
from jax.experimental.pallas import tpu as pltpu
from jax.sharding import PartitionSpec as P

CAP = 2
BIG = 0x7FFFFFFF


def iota(shape, axis):
    return lax.broadcasted_iota(jnp.int32, shape, axis)


def request_kernel(neighbors_ref, keys_ref):
    box_count, column_count = neighbors_ref.shape
    groups = keys_ref.shape[0]
    myself = lax.axis_index("box").astype(jnp.int32)
    peer = iota((groups, column_count), 0)
    column = iota((groups, column_count), 1)
    first = jnp.full((groups, column_count), BIG, jnp.int32)
    last = jnp.full((groups, column_count), -1, jnp.int32)
    for home in range(box_count):
        named = neighbors_ref[home : home + 1, :]
        owner = jnp.where(named >= 0, named >> 4, -1)
        owner = jnp.where(owner == myself, -1, owner)
        key = ((home * column_count + column) << 16) | (column << 8) | (home << 4) | (named & 15)
        member = jnp.broadcast_to(owner, peer.shape) == peer
        first = jnp.minimum(first, jnp.where(member, key, BIG))
        last = jnp.maximum(last, jnp.where(member, key, -1))
    first = jnp.min(first, axis=1, keepdims=True)
    last = jnp.max(last, axis=1, keepdims=True)
    last = jnp.where(last == first, -1, last)
    first = jnp.where(first == BIG, -1, first)
    lane = iota(keys_ref.shape, 1)
    keys_ref[...] = jnp.where(lane == 0, first, jnp.where(lane == 1, last, -1))


def pack_kernel(operators_ref, packed_ref):
    blocks = [operators_ref[16 * i : 16 * (i + 1), :] for i in range(6)]
    pad = jnp.zeros((16, 32), operators_ref.dtype)
    row = jnp.concatenate(blocks + [pad], axis=1)
    for i in range(packed_ref.shape[0]):
        packed_ref[i] = row


def expand(rows, modulo):
    lane = iota((128, 1536), 1)
    row = iota((128, 1536), 0)
    pick = ((lane >> 8) << 4) + ((lane & 15) if modulo else ((lane >> 4) & 15))
    ones = jnp.where(pick == row, 1.0, 0.0).astype(jnp.bfloat16)
    return jnp.dot(rows, ones, preferred_element_type=jnp.float32)


def image_kernel(
    packed_ref, coeffs_ref, high_ref, low_ref, outer_ref, inner_ref, left_ref, half_ref, kron_ref
):
    term = lax.axis_index("term").astype(jnp.int32)
    rows = packed_ref[...].reshape(128, 128)
    outer_ref[...] = expand(rows, False)
    inner_ref[...] = expand(rows, True)
    diagonal = (iota((16, 256), 1) & 15) == iota((16, 256), 0)
    for r in range(16):
        d, e = divmod(r, 2)
        for m in range(3):
            lanes = slice(256 * (3 * e + m), 256 * (3 * e + m + 1))
            for al in range(2):
                row = outer_ref[pl.ds(16 * d + 2 * term + al, 1), lanes]
                block = jnp.where(diagonal, jnp.broadcast_to(row, (16, 256)), 0.0)
                at = 96 * r + 32 * m + 16 * al
                left_ref[at : at + 16, :] = block.astype(jnp.bfloat16)
    half = jnp.dot(left_ref[...], coeffs_ref[...], preferred_element_type=jnp.float32)
    half = half.astype(jnp.bfloat16)
    for r in range(16):
        half_ref[:, 256 * r : 256 * (r + 1)] = half[96 * r : 96 * (r + 1), :]
    for n in range(3):
        for p in range(3):
            slot = (3 * n + p) % 2
            for r in range(16):
                d, e = divmod(r, 2)
                at = 3 * e + n
                outer = outer_ref[16 * d : 16 * (d + 1), 256 * at : 256 * (at + 1)]
                at = 3 * e + p
                inner = inner_ref[16 * d : 16 * (d + 1), 256 * at : 256 * (at + 1)]
                product = outer[:, None, :] * inner[None, :, :]
                kron_ref[slot, :, 256 * r : 256 * (r + 1)] = product.reshape(256, 256).astype(
                    jnp.bfloat16
                )
            applied = lax.dot_general(
                half_ref[...],
                kron_ref[slot],
                (((1,), (1,)), ((), ())),
                preferred_element_type=jnp.float32,
            )
            high = applied.astype(jnp.bfloat16)
            low = (applied - high.astype(jnp.float32)).astype(jnp.bfloat16)
            for m in range(3):
                code = 9 * m + 3 * n + p
                for al in range(2):
                    at = 32 * m + 16 * al
                    to = (slice(16 * code, 16 * (code + 1)), slice(256 * al, 256 * (al + 1)))
                    high_ref[to] = high[at : at + 16, :]
                    low_ref[to] = low[at : at + 16, :]


def message_kernel(keys_ref, guests_ref, high_ref, message_ref, chunk_ref):
    spots = []
    for slot in range(CAP):
        key = keys_ref[:, slot : slot + 1]
        spot = (12 - ((key >> 8) & 15)) * 16 + ((key >> 4) & 15)
        spots.append(jnp.where(key < 0, -1, spot))
    for slot in range(CAP):
        key = guests_ref[:, slot : slot + 1]
        spot = (14 + ((key >> 8) & 15)) * 16 + (key & 15)
        spots.append(jnp.where(key < 0, -1, spot))
    lane = iota((32, 432), 1)
    picks = jnp.concatenate(
        [jnp.where(lane == spot, 1.0, 0.0).astype(jnp.bfloat16) for spot in spots], axis=0
    )
    picked = jnp.dot(picks, high_ref[...], preferred_element_type=jnp.float32)
    for slot in range(2 * CAP):
        for part in range(4):
            chunk_ref[:, 4 * part + slot, :] = picked[
                32 * slot : 32 * (slot + 1), 128 * part : 128 * (part + 1)
            ]
    message_ref[...] = chunk_ref[...].astype(jnp.bfloat16)


def local_kernel(keys_ref, guests_ref, neighbors_ref, high_ref, low_ref, local_ref, place_ref):
    myself = lax.axis_index("box").astype(jnp.int32)
    named = neighbors_ref[...]
    within = named - 16 * myself
    within = jnp.where((within >= 0) & (within < 16), within, -1).astype(jnp.float32)
    within = within.astype(jnp.bfloat16)
    lane = iota((13, 208), 1)
    row = iota((13, 208), 0)
    ahead = jnp.where((lane >> 4) == row, 1.0, 0.0).astype(jnp.bfloat16)
    behind = jnp.where((lane >> 4) == 12 - row, 1.0, 0.0).astype(jnp.bfloat16)
    pull = jnp.dot(within, ahead, preferred_element_type=jnp.float32).astype(jnp.int32)
    push = jnp.dot(within, behind, preferred_element_type=jnp.float32)
    lane = iota((16, 208), 1) & 15
    row = iota((16, 208), 0)
    push = jnp.sum(jnp.where(lane == row, push, 0.0), axis=0, keepdims=True).astype(jnp.int32)
    pull_mask = jnp.where(pull == lane, 1.0, 0.0)
    push_mask = jnp.where(jnp.broadcast_to(push, row.shape) == row, 1.0, 0.0)
    same_mask = jnp.where(iota((16, 16), 0) == iota((16, 16), 1), 1.0, 0.0)
    mask = jnp.concatenate([push_mask, same_mask, pull_mask], axis=1).astype(jnp.bfloat16)
    local = jnp.dot(mask, high_ref[...], preferred_element_type=jnp.float32) + jnp.dot(
        mask, low_ref[...], preferred_element_type=jnp.float32
    )
    for part in range(4):
        local_ref[16 * part : 16 * (part + 1), :] = local[:, 128 * part : 128 * (part + 1)]
    lane = iota((32, 128), 1)
    guests = guests_ref[...]
    keys = jnp.where((lane == 2) | (lane == 3), jnp.roll(keys_ref[...], 2, axis=1), -1)
    target = jnp.where(lane < 2, guests & 15, (keys >> 4) & 15)
    target = jnp.where(jnp.where(lane < 2, guests, keys) < 0, -1, target)
    spread = jnp.where((iota((32, 512), 1) >> 4) == iota((32, 512), 0), 1.0, 0.0)
    target = lax.dot_general(
        target.astype(jnp.float32).astype(jnp.bfloat16),
        spread.astype(jnp.bfloat16),
        (((0,), (0,)), ((), ())),
        preferred_element_type=jnp.float32,
    )[:8]
    lane = iota((8, 512), 1)
    target = jnp.sum(
        jnp.where((lane & 3) == iota((8, 512), 0), target, 0.0), axis=0, keepdims=True
    ).astype(jnp.int32)
    lane = iota((64, 512), 1)
    row = iota((64, 512), 0)
    place = (jnp.broadcast_to(target, lane.shape) == (row & 15)) & (((lane >> 2) & 3) == (row >> 4))
    place_ref[...] = jnp.where(place, 1.0, 0.0).astype(jnp.bfloat16)


def gather_kernel(local_ref, place_ref, arrived_ref, out_ref):
    total = local_ref[...] + jnp.dot(
        place_ref[...], arrived_ref[...].reshape(512, 128), preferred_element_type=jnp.float32
    )
    for part in range(4):
        out_ref[part // 2, :, 128 * (part % 2) : 128 * (part % 2 + 1)] = total[
            16 * part : 16 * (part + 1), :
        ]


def call(kernel, outs, scratch, name, *args):
    vmem = pl.BlockSpec(memory_space=pltpu.VMEM)
    return pl.pallas_call(
        kernel,
        out_shape=outs,
        in_specs=[vmem] * len(args),
        out_specs=jax.tree.map(lambda _: vmem, outs),
        scratch_shapes=scratch,
        name=name,
    )(*args)


def near(value):
    return pltpu.with_memory_space_constraint(value, pltpu.VMEM)


def on_device(coeffs, operators, neighbors):
    degree, box_count, plane_size = coeffs.shape
    groups = lax.axis_size("box")
    terms = lax.axis_size("term")
    shape = pltpu.VMEM
    packed = call(
        pack_kernel,
        shape((terms, degree, 128), jnp.bfloat16),
        [],
        "pack",
        operators.reshape(-1, degree),
    )
    packed = lax.all_to_all(packed, "term", split_axis=0, concat_axis=0, tiled=True)
    keys = call(request_kernel, shape((groups, 128), jnp.int32), [], "request", neighbors)
    guests = lax.all_to_all(keys, "box", split_axis=0, concat_axis=0, tiled=True)
    wide = 2 * plane_size
    image = shape((27 * box_count, wide), jnp.bfloat16)
    high, low = call(
        image_kernel,
        (image, image),
        [
            pltpu.VMEM((128, 1536), jnp.float32),
            pltpu.VMEM((128, 1536), jnp.float32),
            pltpu.VMEM((1536, 256), jnp.bfloat16),
            pltpu.VMEM((96, 4096), jnp.bfloat16),
            pltpu.VMEM((2, 256, 4096), jnp.bfloat16),
        ],
        "image",
        near(packed),
        coeffs.reshape(degree * box_count, plane_size),
    )
    message = call(
        message_kernel,
        shape((groups, 16, 128), jnp.bfloat16),
        [pltpu.VMEM((groups, 16, 128), jnp.float32)],
        "message",
        near(keys),
        near(guests),
        near(high),
    )
    arrived = lax.all_to_all(message, "box", split_axis=0, concat_axis=0, tiled=True)
    local, place = call(
        local_kernel,
        (shape((64, 128), jnp.float32), shape((64, 16 * groups), jnp.bfloat16)),
        [],
        "local",
        near(keys),
        near(guests),
        neighbors,
        near(high),
        near(low),
    )
    return call(
        gather_kernel,
        jax.ShapeDtypeStruct((2, box_count, plane_size), jnp.float32),
        [],
        "gather",
        near(local),
        near(place),
        near(arrived),
    )


def solution(mesh):
    placed = (P(None, "box", None), P("term", None, None, None), P("box", None))
    return jax.shard_map(
        on_device, mesh=mesh, in_specs=placed, out_specs=P("term", "box", None), check_vma=False
    )
```

```python
import functools

import jax
import jax.numpy as jnp
from jax import lax
from jax.experimental import pallas as pl
from jax.experimental.pallas import tpu as pltpu
from jax.sharding import PartitionSpec as P

CAP = 2
GROUP = 4
BIG = 0x7FFFFFFF


def iota(shape, axis):
    return lax.broadcasted_iota(jnp.int32, shape, axis)


def request_kernel(neighbors_ref, operators_ref, keys_ref, mine_ref):
    mine_ref[...] = operators_ref[...]
    box_count, column_count = neighbors_ref.shape
    groups = keys_ref.shape[0]
    myself = lax.axis_index("box").astype(jnp.int32)
    peer = iota((groups, column_count), 0)
    column = iota((groups, column_count), 1)
    first = jnp.full((groups, column_count), BIG, jnp.int32)
    last = jnp.full((groups, column_count), -1, jnp.int32)
    for home in range(box_count):
        named = neighbors_ref[home : home + 1, :]
        owner = jnp.where(named >= 0, named >> 4, -1)
        owner = jnp.where(owner == myself, -1, owner)
        key = ((home * column_count + column) << 16) | (column << 8) | (home << 4) | (named & 15)
        member = jnp.broadcast_to(owner, peer.shape) == peer
        first = jnp.minimum(first, jnp.where(member, key, BIG))
        last = jnp.maximum(last, jnp.where(member, key, -1))
    first = jnp.min(first, axis=1, keepdims=True)
    last = jnp.max(last, axis=1, keepdims=True)
    last = jnp.where(last == first, -1, last)
    first = jnp.where(first == BIG, -1, first)
    lane = iota(keys_ref.shape, 1)
    keys_ref[...] = jnp.where(lane == 0, first, jnp.where(lane == 1, last, -1))


def image_kernel(terms, pieces, first, final, coeffs_ref, *refs):
    rows_refs, refs = refs[:pieces], list(refs[pieces:])
    before_ref = None if first else refs.pop(0)
    after_ref = None if final else refs.pop(0)
    high_ref, low_ref = (refs.pop(0), refs.pop(0)) if final else (None, None)
    outer_ref, inner_ref, left_ref, half_ref, kron_ref = refs[:5]
    sum_ref = refs[5] if final else after_ref
    term = lax.axis_index("term").astype(jnp.int32)
    lane = iota((16, 256), 1)
    row = iota((16, 256), 0)
    to_outer = jnp.where((lane >> 4) == row, 1.0, 0.0).astype(jnp.bfloat16)
    to_inner = jnp.where((lane & 15) == row, 1.0, 0.0).astype(jnp.bfloat16)
    rows = jnp.concatenate([ref[...] for ref in rows_refs], axis=0)
    outer_ref[...] = jnp.dot(rows, to_outer, preferred_element_type=jnp.float32)
    inner_ref[...] = jnp.dot(rows, to_inner, preferred_element_type=jnp.float32).astype(
        jnp.bfloat16
    )
    diagonal = (lane & 15) == row
    for r in range(terms):
        for m in range(3):
            for al in range(2):
                line = outer_ref[pl.ds(16 * (3 * r + m) + 2 * term + al, 1), :]
                block = jnp.where(diagonal, jnp.broadcast_to(line, (16, 256)), 0.0)
                at = 96 * r + 32 * m + 16 * al
                left_ref[at : at + 16, :] = block.astype(jnp.bfloat16)
    half = jnp.dot(left_ref[...], coeffs_ref[...], preferred_element_type=jnp.float32)
    half = half.astype(jnp.bfloat16)
    for r in range(terms):
        half_ref[:, 256 * r : 256 * (r + 1)] = half[96 * r : 96 * (r + 1), :]
    wide = 256 * GROUP
    for start in range(0, terms, GROUP):
        last = start + GROUP == terms
        for n in range(3):
            slot = 3 * ((3 * (start // GROUP) + n) % 2)
            for r in range(start, start + GROUP):
                to = slice(256 * (r - start), 256 * (r - start + 1))
                inner = [
                    inner_ref[16 * (3 * r + p) : 16 * (3 * r + p + 1), :] for p in range(3)
                ]
                for a in range(16):
                    at = 16 * (3 * r + n) + a
                    line = outer_ref[at : at + 1, :]
                    line = jnp.broadcast_to(line, (16, 256)).astype(jnp.bfloat16)
                    for p in range(3):
                        kron_ref[slot + p, 16 * a : 16 * (a + 1), to] = line * inner[p]
            for p in range(3):
                applied = lax.dot_general(
                    half_ref[:, 256 * start : 256 * start + wide],
                    kron_ref[slot + p],
                    (((1,), (1,)), ((), ())),
                    preferred_element_type=jnp.float32,
                )
                if start:
                    applied = applied + sum_ref[3 * n + p]
                elif not first:
                    applied = applied + before_ref[3 * n + p]
                if not (final and last):
                    sum_ref[3 * n + p] = applied
                    continue
                high = applied.astype(jnp.bfloat16)
                low = (applied - high.astype(jnp.float32)).astype(jnp.bfloat16)
                for m in range(3):
                    code = 9 * m + 3 * n + p
                    for al in range(2):
                        at = 32 * m + 16 * al
                        to = (slice(16 * code, 16 * (code + 1)), slice(256 * al, 256 * (al + 1)))
                        high_ref[to] = high[at : at + 16, :]
                        low_ref[to] = low[at : at + 16, :]


def message_kernel(keys_ref, guests_ref, high_ref, message_ref, chunk_ref):
    spots = []
    for slot in range(CAP):
        key = keys_ref[:, slot : slot + 1]
        spot = (12 - ((key >> 8) & 15)) * 16 + ((key >> 4) & 15)
        spots.append(jnp.where(key < 0, -1, spot))
    for slot in range(CAP):
        key = guests_ref[:, slot : slot + 1]
        spot = (14 + ((key >> 8) & 15)) * 16 + (key & 15)
        spots.append(jnp.where(key < 0, -1, spot))
    lane = iota((32, 432), 1)
    picks = jnp.concatenate(
        [jnp.where(lane == spot, 1.0, 0.0).astype(jnp.bfloat16) for spot in spots], axis=0
    )
    picked = jnp.dot(picks, high_ref[...], preferred_element_type=jnp.float32)
    for slot in range(2 * CAP):
        for part in range(4):
            chunk_ref[:, 4 * part + slot, :] = picked[
                32 * slot : 32 * (slot + 1), 128 * part : 128 * (part + 1)
            ]
    message_ref[...] = chunk_ref[...].astype(jnp.bfloat16)


def local_kernel(keys_ref, guests_ref, neighbors_ref, high_ref, low_ref, local_ref, place_ref):
    myself = lax.axis_index("box").astype(jnp.int32)
    named = neighbors_ref[...]
    within = named - 16 * myself
    within = jnp.where((within >= 0) & (within < 16), within, -1).astype(jnp.float32)
    within = within.astype(jnp.bfloat16)
    lane = iota((13, 208), 1)
    row = iota((13, 208), 0)
    ahead = jnp.where((lane >> 4) == row, 1.0, 0.0).astype(jnp.bfloat16)
    behind = jnp.where((lane >> 4) == 12 - row, 1.0, 0.0).astype(jnp.bfloat16)
    pull = jnp.dot(within, ahead, preferred_element_type=jnp.float32).astype(jnp.int32)
    push = jnp.dot(within, behind, preferred_element_type=jnp.float32)
    lane = iota((16, 208), 1) & 15
    row = iota((16, 208), 0)
    push = jnp.sum(jnp.where(lane == row, push, 0.0), axis=0, keepdims=True).astype(jnp.int32)
    pull_mask = jnp.where(pull == lane, 1.0, 0.0)
    push_mask = jnp.where(jnp.broadcast_to(push, row.shape) == row, 1.0, 0.0)
    same_mask = jnp.where(iota((16, 16), 0) == iota((16, 16), 1), 1.0, 0.0)
    mask = jnp.concatenate([push_mask, same_mask, pull_mask], axis=1).astype(jnp.bfloat16)
    local = jnp.dot(mask, high_ref[...], preferred_element_type=jnp.float32) + jnp.dot(
        mask, low_ref[...], preferred_element_type=jnp.float32
    )
    for part in range(4):
        local_ref[16 * part : 16 * (part + 1), :] = local[:, 128 * part : 128 * (part + 1)]
    lane = iota((32, 128), 1)
    guests = guests_ref[...]
    keys = jnp.where((lane == 2) | (lane == 3), jnp.roll(keys_ref[...], 2, axis=1), -1)
    target = jnp.where(lane < 2, guests & 15, (keys >> 4) & 15)
    target = jnp.where(jnp.where(lane < 2, guests, keys) < 0, -1, target)
    spread = jnp.where((iota((32, 512), 1) >> 4) == iota((32, 512), 0), 1.0, 0.0)
    target = lax.dot_general(
        target.astype(jnp.float32).astype(jnp.bfloat16),
        spread.astype(jnp.bfloat16),
        (((0,), (0,)), ((), ())),
        preferred_element_type=jnp.float32,
    )[:8]
    lane = iota((8, 512), 1)
    target = jnp.sum(
        jnp.where((lane & 3) == iota((8, 512), 0), target, 0.0), axis=0, keepdims=True
    ).astype(jnp.int32)
    lane = iota((64, 512), 1)
    row = iota((64, 512), 0)
    place = (jnp.broadcast_to(target, lane.shape) == (row & 15)) & (((lane >> 2) & 3) == (row >> 4))
    place_ref[...] = jnp.where(place, 1.0, 0.0).astype(jnp.bfloat16)


def gather_kernel(local_ref, place_ref, arrived_ref, out_ref):
    total = local_ref[...] + jnp.dot(
        place_ref[...], arrived_ref[...].reshape(512, 128), preferred_element_type=jnp.float32
    )
    for part in range(4):
        out_ref[part // 2, :, 128 * (part % 2) : 128 * (part % 2 + 1)] = total[
            16 * part : 16 * (part + 1), :
        ]


def call(kernel, outs, scratch, *args):
    vmem = pl.BlockSpec(memory_space=pltpu.VMEM)
    return pl.pallas_call(
        kernel,
        out_shape=outs,
        in_specs=[vmem] * len(args),
        out_specs=jax.tree.map(lambda _: vmem, outs),
        scratch_shapes=scratch,
    )(*args)


def near(value):
    return pltpu.with_memory_space_constraint(value, pltpu.VMEM)


def on_device(coeffs, operators, neighbors):
    degree, box_count, plane_size = coeffs.shape
    groups = lax.axis_size("box")
    terms = lax.axis_size("term")
    shape = pltpu.VMEM
    coeffs = near(coeffs.reshape(degree * box_count, plane_size))
    totals = shape((9, 6 * box_count, plane_size), jnp.float32)
    image = shape((27 * box_count, 2 * plane_size), jnp.bfloat16)

    def swap(value, bit):
        return lax.ppermute(value, "term", [(i, i ^ bit) for i in range(terms)])

    def images(rows, before, final):
        height = sum(piece.shape[0] for piece in rows)
        count = height // (3 * degree)
        scratch = [
            pltpu.VMEM((height, plane_size), jnp.float32),
            pltpu.VMEM((height, plane_size), jnp.bfloat16),
            pltpu.VMEM((6 * box_count * count, plane_size), jnp.bfloat16),
            pltpu.VMEM((6 * box_count, plane_size * count), jnp.bfloat16),
            pltpu.VMEM((6, plane_size, plane_size * GROUP), jnp.bfloat16),
        ]
        if final:
            scratch.append(pltpu.VMEM((9, 6 * box_count, plane_size), jnp.float32))
        return call(
            functools.partial(image_kernel, count, len(rows), before is None, final),
            (image, image) if final else totals,
            scratch,
            coeffs,
            *[near(piece) for piece in rows],
            *([] if before is None else [near(before)]),
        )

    mine = operators.reshape(-1, degree)
    other = swap(mine, 4)
    keys, pair = call(
        request_kernel,
        (shape((groups, 128), jnp.int32), shape(mine.shape, mine.dtype)),
        [],
        neighbors,
        mine,
    )
    guests = lax.all_to_all(keys, "box", split_axis=0, concat_axis=0, tiled=True)
    pair = jnp.concatenate([pair, other], axis=0)
    ones = swap(pair, 1)
    twos = swap(pair, 2)
    threes = swap(pair, 3)
    total = images([pair], None, False)
    total = images([ones], total, False)
    high, low = images([twos, threes], total, True)
    message = call(
        message_kernel,
        shape((groups, 16, 128), jnp.bfloat16),
        [pltpu.VMEM((groups, 16, 128), jnp.float32)],
        near(keys),
        near(guests),
        near(high),
    )
    arrived = lax.all_to_all(message, "box", split_axis=0, concat_axis=0, tiled=True)
    local, place = call(
        local_kernel,
        (shape((64, 128), jnp.float32), shape((64, 16 * groups), jnp.bfloat16)),
        [],
        near(keys),
        near(guests),
        neighbors,
        near(high),
        near(low),
    )
    return call(
        gather_kernel,
        jax.ShapeDtypeStruct((2, box_count, plane_size), jnp.float32),
        [],
        near(local),
        near(place),
        near(arrived),
    )


def solution(mesh):
    placed = (P(None, "box", None), P("term", None, None, None), P("box", None))
    return jax.shard_map(
        on_device, mesh=mesh, in_specs=placed, out_specs=P("term", "box", None), check_vma=False
    )
```

```python
import functools

import jax
import jax.numpy as jnp
from jax import lax
from jax.experimental import pallas as pl
from jax.experimental.pallas import tpu as pltpu
from jax.sharding import PartitionSpec as P

CAP = 2
GROUP = 4
BIG = 0x7FFFFFFF


def iota(shape, axis):
    return lax.broadcasted_iota(jnp.int32, shape, axis)


def request_kernel(neighbors_ref, operators_ref, keys_ref, mine_ref):
    mine_ref[...] = operators_ref[...]
    box_count, column_count = neighbors_ref.shape
    groups = keys_ref.shape[0]
    myself = lax.axis_index("box").astype(jnp.int32)
    peer = iota((groups, column_count), 0)
    column = iota((groups, column_count), 1)
    first = jnp.full((groups, column_count), BIG, jnp.int32)
    last = jnp.full((groups, column_count), -1, jnp.int32)
    for home in range(box_count):
        named = neighbors_ref[home : home + 1, :]
        owner = jnp.where(named >= 0, named >> 4, -1)
        owner = jnp.where(owner == myself, -1, owner)
        key = ((home * column_count + column) << 16) | (column << 8) | (home << 4) | (named & 15)
        member = jnp.broadcast_to(owner, peer.shape) == peer
        first = jnp.minimum(first, jnp.where(member, key, BIG))
        last = jnp.maximum(last, jnp.where(member, key, -1))
    first = jnp.min(first, axis=1, keepdims=True)
    last = jnp.max(last, axis=1, keepdims=True)
    last = jnp.where(last == first, -1, last)
    first = jnp.where(first == BIG, -1, first)
    lane = iota(keys_ref.shape, 1)
    keys_ref[...] = jnp.where(lane == 0, first, jnp.where(lane == 1, last, -1))


def image_kernel(terms, pieces, first, final, coeffs_ref, *refs):
    rows_refs, refs = refs[:pieces], list(refs[pieces:])
    before_ref = None if first else refs.pop(0)
    after_ref = None if final else refs.pop(0)
    high_ref, low_ref = (refs.pop(0), refs.pop(0)) if final else (None, None)
    outer_ref, inner_ref, left_ref, half_ref, kron_ref = refs[:5]
    sum_ref = refs[5] if final else after_ref
    term = lax.axis_index("term").astype(jnp.int32)
    lane = iota((16, 256), 1)
    row = iota((16, 256), 0)
    to_outer = jnp.where((lane >> 4) == row, 1.0, 0.0).astype(jnp.bfloat16)
    to_inner = jnp.where((lane & 15) == row, 1.0, 0.0).astype(jnp.bfloat16)
    rows = jnp.concatenate([ref[...] for ref in rows_refs], axis=0)
    outer_ref[...] = jnp.dot(rows, to_outer, preferred_element_type=jnp.float32)
    inner_ref[...] = jnp.dot(rows, to_inner, preferred_element_type=jnp.float32).astype(
        jnp.bfloat16
    )
    diagonal = (lane & 15) == row
    for r in range(terms):
        for m in range(3):
            for al in range(2):
                line = outer_ref[pl.ds(16 * (3 * r + m) + 2 * term + al, 1), :]
                block = jnp.where(diagonal, jnp.broadcast_to(line, (16, 256)), 0.0)
                at = 96 * r + 32 * m + 16 * al
                left_ref[at : at + 16, :] = block.astype(jnp.bfloat16)
    half = jnp.dot(left_ref[...], coeffs_ref[...], preferred_element_type=jnp.float32)
    half = half.astype(jnp.bfloat16)
    for r in range(terms):
        half_ref[:, 256 * r : 256 * (r + 1)] = half[96 * r : 96 * (r + 1), :]
    wide = 256 * GROUP
    for start in range(0, terms, GROUP):
        last = start + GROUP == terms
        for n in range(3):
            slot = 3 * ((3 * (start // GROUP) + n) % 2)
            for r in range(start, start + GROUP):
                to = slice(256 * (r - start), 256 * (r - start + 1))
                inner = [
                    inner_ref[16 * (3 * r + p) : 16 * (3 * r + p + 1), :] for p in range(3)
                ]
                for a in range(16):
                    at = 16 * (3 * r + n) + a
                    line = outer_ref[at : at + 1, :]
                    line = jnp.broadcast_to(line, (16, 256)).astype(jnp.bfloat16)
                    for p in range(3):
                        kron_ref[slot + p, 16 * a : 16 * (a + 1), to] = line * inner[p]
            for p in range(3):
                applied = lax.dot_general(
                    half_ref[:, 256 * start : 256 * start + wide],
                    kron_ref[slot + p],
                    (((1,), (1,)), ((), ())),
                    preferred_element_type=jnp.float32,
                )
                if start:
                    applied = applied + sum_ref[3 * n + p]
                elif not first:
                    applied = applied + before_ref[3 * n + p]
                if not (final and last):
                    sum_ref[3 * n + p] = applied
                    continue
                high = applied.astype(jnp.bfloat16)
                low = (applied - high.astype(jnp.float32)).astype(jnp.bfloat16)
                for m in range(3):
                    code = 9 * m + 3 * n + p
                    for al in range(2):
                        at = 32 * m + 16 * al
                        to = (slice(16 * code, 16 * (code + 1)), slice(256 * al, 256 * (al + 1)))
                        high_ref[to] = high[at : at + 16, :]
                        low_ref[to] = low[at : at + 16, :]


def message_kernel(
    keys_ref,
    guests_ref,
    neighbors_ref,
    high_ref,
    low_ref,
    message_ref,
    local_ref,
    place_ref,
    chunk_ref,
):
    spots = []
    for slot in range(CAP):
        key = keys_ref[:, slot : slot + 1]
        spot = (12 - ((key >> 8) & 15)) * 16 + ((key >> 4) & 15)
        spots.append(jnp.where(key < 0, -1, spot))
    for slot in range(CAP):
        key = guests_ref[:, slot : slot + 1]
        spot = (14 + ((key >> 8) & 15)) * 16 + (key & 15)
        spots.append(jnp.where(key < 0, -1, spot))
    lane = iota((32, 432), 1)
    picks = jnp.concatenate(
        [jnp.where(lane == spot, 1.0, 0.0).astype(jnp.bfloat16) for spot in spots], axis=0
    )
    picked = jnp.dot(picks, high_ref[...], preferred_element_type=jnp.float32)
    for slot in range(2 * CAP):
        for part in range(4):
            chunk_ref[:, 4 * part + slot, :] = picked[
                32 * slot : 32 * (slot + 1), 128 * part : 128 * (part + 1)
            ]
    message_ref[...] = chunk_ref[...].astype(jnp.bfloat16)
    myself = lax.axis_index("box").astype(jnp.int32)
    named = neighbors_ref[...]
    within = named - 16 * myself
    within = jnp.where((within >= 0) & (within < 16), within, -1).astype(jnp.float32)
    within = within.astype(jnp.bfloat16)
    lane = iota((13, 208), 1)
    row = iota((13, 208), 0)
    ahead = jnp.where((lane >> 4) == row, 1.0, 0.0).astype(jnp.bfloat16)
    behind = jnp.where((lane >> 4) == 12 - row, 1.0, 0.0).astype(jnp.bfloat16)
    pull = jnp.dot(within, ahead, preferred_element_type=jnp.float32).astype(jnp.int32)
    push = jnp.dot(within, behind, preferred_element_type=jnp.float32)
    lane = iota((16, 208), 1) & 15
    row = iota((16, 208), 0)
    push = jnp.sum(jnp.where(lane == row, push, 0.0), axis=0, keepdims=True).astype(jnp.int32)
    pull_mask = jnp.where(pull == lane, 1.0, 0.0)
    push_mask = jnp.where(jnp.broadcast_to(push, row.shape) == row, 1.0, 0.0)
    same_mask = jnp.where(iota((16, 16), 0) == iota((16, 16), 1), 1.0, 0.0)
    mask = jnp.concatenate([push_mask, same_mask, pull_mask], axis=1).astype(jnp.bfloat16)
    local = jnp.dot(mask, high_ref[...], preferred_element_type=jnp.float32) + jnp.dot(
        mask, low_ref[...], preferred_element_type=jnp.float32
    )
    for part in range(4):
        local_ref[16 * part : 16 * (part + 1), :] = local[:, 128 * part : 128 * (part + 1)]
    lane = iota((32, 128), 1)
    guests = guests_ref[...]
    keys = jnp.where((lane == 2) | (lane == 3), jnp.roll(keys_ref[...], 2, axis=1), -1)
    target = jnp.where(lane < 2, guests & 15, (keys >> 4) & 15)
    target = jnp.where(jnp.where(lane < 2, guests, keys) < 0, -1, target)
    spread = jnp.where((iota((32, 512), 1) >> 4) == iota((32, 512), 0), 1.0, 0.0)
    target = lax.dot_general(
        target.astype(jnp.float32).astype(jnp.bfloat16),
        spread.astype(jnp.bfloat16),
        (((0,), (0,)), ((), ())),
        preferred_element_type=jnp.float32,
    )[:8]
    lane = iota((8, 512), 1)
    target = jnp.sum(
        jnp.where((lane & 3) == iota((8, 512), 0), target, 0.0), axis=0, keepdims=True
    ).astype(jnp.int32)
    lane = iota((64, 512), 1)
    row = iota((64, 512), 0)
    place = (jnp.broadcast_to(target, lane.shape) == (row & 15)) & (((lane >> 2) & 3) == (row >> 4))
    place_ref[...] = jnp.where(place, 1.0, 0.0).astype(jnp.bfloat16)


def gather_kernel(local_ref, place_ref, arrived_ref, out_ref):
    total = local_ref[...] + jnp.dot(
        place_ref[...], arrived_ref[...].reshape(512, 128), preferred_element_type=jnp.float32
    )
    for part in range(4):
        out_ref[part // 2, :, 128 * (part % 2) : 128 * (part % 2 + 1)] = total[
            16 * part : 16 * (part + 1), :
        ]


def call(kernel, outs, scratch, *args):
    vmem = pl.BlockSpec(memory_space=pltpu.VMEM)
    return pl.pallas_call(
        kernel,
        out_shape=outs,
        in_specs=[vmem] * len(args),
        out_specs=jax.tree.map(lambda _: vmem, outs),
        scratch_shapes=scratch,
    )(*args)


def near(value):
    return pltpu.with_memory_space_constraint(value, pltpu.VMEM)


def on_device(coeffs, operators, neighbors):
    degree, box_count, plane_size = coeffs.shape
    groups = lax.axis_size("box")
    terms = lax.axis_size("term")
    shape = pltpu.VMEM
    coeffs = near(coeffs.reshape(degree * box_count, plane_size))
    totals = shape((9, 6 * box_count, plane_size), jnp.float32)
    image = shape((27 * box_count, 2 * plane_size), jnp.bfloat16)

    def swap(value, other):
        return lax.ppermute(value, "term", [(i, other(i) % terms) for i in range(terms)])

    def images(rows, before, final):
        height = sum(piece.shape[0] for piece in rows)
        count = height // (3 * degree)
        scratch = [
            pltpu.VMEM((height, plane_size), jnp.float32),
            pltpu.VMEM((height, plane_size), jnp.bfloat16),
            pltpu.VMEM((6 * box_count * count, plane_size), jnp.bfloat16),
            pltpu.VMEM((6 * box_count, plane_size * count), jnp.bfloat16),
            pltpu.VMEM((6, plane_size, plane_size * GROUP), jnp.bfloat16),
        ]
        if final:
            scratch.append(pltpu.VMEM((9, 6 * box_count, plane_size), jnp.float32))
        return call(
            functools.partial(image_kernel, count, len(rows), before is None, final),
            (image, image) if final else totals,
            scratch,
            coeffs,
            *[near(piece) for piece in rows],
            *([] if before is None else [near(before)]),
        )

    mine = operators.reshape(-1, degree)
    other = swap(mine, lambda i: i ^ 4)
    keys, pair = call(
        request_kernel,
        (shape((groups, 128), jnp.int32), shape(mine.shape, mine.dtype)),
        [],
        neighbors,
        mine,
    )
    guests = lax.all_to_all(keys, "box", split_axis=0, concat_axis=0, tiled=True)
    pair = jnp.concatenate([pair, other], axis=0)
    ones = swap(pair, lambda i: i ^ 1)
    twos = swap(pair, lambda i: i ^ 2)
    threes = swap(pair, lambda i: i + (1 if i % 2 else -1))
    total = images([pair], None, False)
    total = images([ones], total, False)
    high, low = images([twos, threes], total, True)
    message, local, place = call(
        message_kernel,
        (
            shape((groups, 16, 128), jnp.bfloat16),
            shape((64, 128), jnp.float32),
            shape((64, 16 * groups), jnp.bfloat16),
        ),
        [pltpu.VMEM((groups, 16, 128), jnp.float32)],
        near(keys),
        near(guests),
        near(neighbors),
        near(high),
        near(low),
    )
    arrived = lax.all_to_all(message, "box", split_axis=0, concat_axis=0, tiled=True)
    return call(
        gather_kernel,
        jax.ShapeDtypeStruct((2, box_count, plane_size), jnp.float32),
        [],
        near(local),
        near(place),
        near(arrived),
    )


def solution(mesh):
    placed = (P(None, "box", None), P("term", None, None, None), P("box", None))
    return jax.shard_map(
        on_device, mesh=mesh, in_specs=placed, out_specs=P("term", "box", None), check_vma=False
    )
```

```python
import functools

import jax
import jax.numpy as jnp
from jax import lax
from jax.experimental import pallas as pl
from jax.experimental.pallas import tpu as pltpu
from jax.sharding import PartitionSpec as P

CAP = 2
GROUP = 4
BIG = 0x7FFFFFFF


def iota(shape, axis):
    return lax.broadcasted_iota(jnp.int32, shape, axis)


def request_kernel(
    neighbors_hbm,
    operators_hbm,
    coeffs_hbm,
    keys_ref,
    mine_ref,
    near_ref,
    neighbors_ref,
    operators_ref,
    arrivals,
):
    fetches = [
        pltpu.make_async_copy(source, target, arrivals.at[i])
        for i, (source, target) in enumerate(
            (
                (neighbors_hbm, neighbors_ref),
                (operators_hbm, operators_ref),
                (coeffs_hbm, near_ref),
            )
        )
    ]
    for fetch in fetches:
        fetch.start()
    fetches[1].wait()
    blocks = [operators_ref[16 * i : 16 * (i + 1), :] for i in range(6)]
    pad = jnp.zeros((16, 32), operators_ref.dtype)
    mine_ref[0] = jnp.concatenate(blocks + [pad], axis=1)
    fetches[0].wait()
    box_count, column_count = neighbors_ref.shape
    groups = keys_ref.shape[0]
    myself = lax.axis_index("box").astype(jnp.int32)
    peer = iota((groups, column_count), 0)
    column = iota((groups, column_count), 1)
    first = jnp.full((groups, column_count), BIG, jnp.int32)
    last = jnp.full((groups, column_count), -1, jnp.int32)
    for home in range(box_count):
        named = neighbors_ref[home : home + 1, :]
        owner = jnp.where(named >= 0, named >> 4, -1)
        owner = jnp.where(owner == myself, -1, owner)
        key = ((home * column_count + column) << 16) | (column << 8) | (home << 4) | (named & 15)
        member = jnp.broadcast_to(owner, peer.shape) == peer
        first = jnp.minimum(first, jnp.where(member, key, BIG))
        last = jnp.maximum(last, jnp.where(member, key, -1))
    first = jnp.min(first, axis=1, keepdims=True)
    last = jnp.max(last, axis=1, keepdims=True)
    last = jnp.where(last == first, -1, last)
    first = jnp.where(first == BIG, -1, first)
    lane = iota(keys_ref.shape, 1)
    keys_ref[...] = jnp.where(lane == 0, first, jnp.where(lane == 1, last, -1))
    fetches[2].wait()


def image_kernel(terms, pieces, first, final, coeffs_ref, *refs):
    rows_refs, refs = refs[:pieces], list(refs[pieces:])
    before_ref = None if first else refs.pop(0)
    after_ref = None if final else refs.pop(0)
    high_ref, low_ref = (refs.pop(0), refs.pop(0)) if final else (None, None)
    outer_ref, inner_ref, left_ref, half_ref, kron_ref = refs[:5]
    sum_ref = refs[5] if final else after_ref
    term = lax.axis_index("term").astype(jnp.int32)
    lane = iota((16, 256), 1)
    row = iota((16, 256), 0)
    to_outer = jnp.where((lane >> 4) == row, 1.0, 0.0).astype(jnp.bfloat16)
    to_inner = jnp.where((lane & 15) == row, 1.0, 0.0).astype(jnp.bfloat16)
    blocks = []
    for ref in rows_refs:
        for i in range(ref.shape[0]):
            packed = ref[i]
            blocks += [packed[:, 16 * b : 16 * (b + 1)] for b in range(6)]
    rows = jnp.concatenate(blocks, axis=0)
    outer_ref[...] = jnp.dot(rows, to_outer, preferred_element_type=jnp.float32)
    inner_ref[...] = jnp.dot(rows, to_inner, preferred_element_type=jnp.float32).astype(
        jnp.bfloat16
    )
    diagonal = (lane & 15) == row
    for r in range(terms):
        for m in range(3):
            for al in range(2):
                line = outer_ref[pl.ds(16 * (3 * r + m) + 2 * term + al, 1), :]
                block = jnp.where(diagonal, jnp.broadcast_to(line, (16, 256)), 0.0)
                at = 96 * r + 32 * m + 16 * al
                left_ref[at : at + 16, :] = block.astype(jnp.bfloat16)
    half = jnp.dot(left_ref[...], coeffs_ref[...], preferred_element_type=jnp.float32)
    half = half.astype(jnp.bfloat16)
    for r in range(terms):
        half_ref[:, 256 * r : 256 * (r + 1)] = half[96 * r : 96 * (r + 1), :]
    wide = 256 * GROUP
    for start in range(0, terms, GROUP):
        last = start + GROUP == terms
        for n in range(3):
            slot = 3 * ((3 * (start // GROUP) + n) % 2)
            for r in range(start, start + GROUP):
                to = slice(256 * (r - start), 256 * (r - start + 1))
                inner = [
                    inner_ref[16 * (3 * r + p) : 16 * (3 * r + p + 1), :] for p in range(3)
                ]
                for a in range(16):
                    at = 16 * (3 * r + n) + a
                    line = outer_ref[at : at + 1, :]
                    line = jnp.broadcast_to(line, (16, 256)).astype(jnp.bfloat16)
                    for p in range(3):
                        kron_ref[slot + p, 16 * a : 16 * (a + 1), to] = line * inner[p]
            for p in range(3):
                applied = lax.dot_general(
                    half_ref[:, 256 * start : 256 * start + wide],
                    kron_ref[slot + p],
                    (((1,), (1,)), ((), ())),
                    preferred_element_type=jnp.float32,
                )
                if start:
                    applied = applied + sum_ref[3 * n + p]
                elif not first:
                    applied = applied + before_ref[3 * n + p]
                if not (final and last):
                    sum_ref[3 * n + p] = applied
                    continue
                high = applied.astype(jnp.bfloat16)
                low = (applied - high.astype(jnp.float32)).astype(jnp.bfloat16)
                for m in range(3):
                    code = 9 * m + 3 * n + p
                    for al in range(2):
                        at = 32 * m + 16 * al
                        to = (slice(16 * code, 16 * (code + 1)), slice(256 * al, 256 * (al + 1)))
                        high_ref[to] = high[at : at + 16, :]
                        low_ref[to] = low[at : at + 16, :]


def flip_of(groups):
    return groups // 2 + groups // 8


def flipped(rows):
    groups = rows.shape[0]
    part = groups // 8
    flip = flip_of(groups) // part
    return jnp.concatenate(
        [rows[part * (i ^ flip) : part * ((i ^ flip) + 1), :] for i in range(8)], axis=0
    )


def message_kernel(
    keys_ref,
    guests_ref,
    neighbors_ref,
    high_ref,
    low_ref,
    message_ref,
    local_ref,
    place_ref,
    chunk_ref,
):
    keys = flipped(keys_ref[...])
    guests = flipped(guests_ref[...])
    spots = []
    for slot in range(CAP):
        key = keys[:, slot : slot + 1]
        spot = (12 - ((key >> 8) & 15)) * 16 + ((key >> 4) & 15)
        spots.append(jnp.where(key < 0, -1, spot))
    for slot in range(CAP):
        key = guests[:, slot : slot + 1]
        spot = (14 + ((key >> 8) & 15)) * 16 + (key & 15)
        spots.append(jnp.where(key < 0, -1, spot))
    lane = iota((32, 432), 1)
    picks = jnp.concatenate(
        [jnp.where(lane == spot, 1.0, 0.0).astype(jnp.bfloat16) for spot in spots], axis=0
    )
    picked = jnp.dot(picks, high_ref[...], preferred_element_type=jnp.float32)
    for slot in range(2 * CAP):
        for part in range(4):
            chunk_ref[:, 4 * part + slot, :] = picked[
                32 * slot : 32 * (slot + 1), 128 * part : 128 * (part + 1)
            ]
    message_ref[...] = chunk_ref[...].astype(jnp.bfloat16)
    myself = lax.axis_index("box").astype(jnp.int32)
    named = neighbors_ref[...]
    within = named - 16 * myself
    within = jnp.where((within >= 0) & (within < 16), within, -1).astype(jnp.float32)
    within = within.astype(jnp.bfloat16)
    lane = iota((13, 208), 1)
    row = iota((13, 208), 0)
    ahead = jnp.where((lane >> 4) == row, 1.0, 0.0).astype(jnp.bfloat16)
    behind = jnp.where((lane >> 4) == 12 - row, 1.0, 0.0).astype(jnp.bfloat16)
    pull = jnp.dot(within, ahead, preferred_element_type=jnp.float32).astype(jnp.int32)
    push = jnp.dot(within, behind, preferred_element_type=jnp.float32)
    lane = iota((16, 208), 1) & 15
    row = iota((16, 208), 0)
    push = jnp.sum(jnp.where(lane == row, push, 0.0), axis=0, keepdims=True).astype(jnp.int32)
    pull_mask = jnp.where(pull == lane, 1.0, 0.0)
    push_mask = jnp.where(jnp.broadcast_to(push, row.shape) == row, 1.0, 0.0)
    same_mask = jnp.where(iota((16, 16), 0) == iota((16, 16), 1), 1.0, 0.0)
    mask = jnp.concatenate([push_mask, same_mask, pull_mask], axis=1).astype(jnp.bfloat16)
    local = jnp.dot(mask, high_ref[...], preferred_element_type=jnp.float32) + jnp.dot(
        mask, low_ref[...], preferred_element_type=jnp.float32
    )
    for part in range(4):
        local_ref[16 * part : 16 * (part + 1), :] = local[:, 128 * part : 128 * (part + 1)]
    lane = iota((32, 128), 1)
    keys = jnp.where((lane == 2) | (lane == 3), jnp.roll(keys, 2, axis=1), -1)
    target = jnp.where(lane < 2, guests & 15, (keys >> 4) & 15)
    target = jnp.where(jnp.where(lane < 2, guests, keys) < 0, -1, target)
    spread = jnp.where((iota((32, 512), 1) >> 4) == iota((32, 512), 0), 1.0, 0.0)
    target = lax.dot_general(
        target.astype(jnp.float32).astype(jnp.bfloat16),
        spread.astype(jnp.bfloat16),
        (((0,), (0,)), ((), ())),
        preferred_element_type=jnp.float32,
    )[:8]
    lane = iota((8, 512), 1)
    target = jnp.sum(
        jnp.where((lane & 3) == iota((8, 512), 0), target, 0.0), axis=0, keepdims=True
    ).astype(jnp.int32)
    lane = iota((64, 512), 1)
    row = iota((64, 512), 0)
    place = (jnp.broadcast_to(target, lane.shape) == (row & 15)) & (((lane >> 2) & 3) == (row >> 4))
    place_ref[...] = jnp.where(place, 1.0, 0.0).astype(jnp.bfloat16)


def gather_kernel(local_ref, place_ref, arrived_ref, out_ref):
    total = local_ref[...] + jnp.dot(
        place_ref[...], arrived_ref[...].reshape(512, 128), preferred_element_type=jnp.float32
    )
    for part in range(4):
        out_ref[part // 2, :, 128 * (part % 2) : 128 * (part % 2 + 1)] = total[
            16 * part : 16 * (part + 1), :
        ]


def call(kernel, outs, scratch, *args, place=pltpu.VMEM):
    vmem = pl.BlockSpec(memory_space=pltpu.VMEM)
    return pl.pallas_call(
        kernel,
        out_shape=outs,
        in_specs=[pl.BlockSpec(memory_space=place)] * len(args),
        out_specs=jax.tree.map(lambda _: vmem, outs),
        scratch_shapes=scratch,
    )(*args)


def near(value):
    return pltpu.with_memory_space_constraint(value, pltpu.VMEM)


def on_device(coeffs, operators, neighbors):
    degree, box_count, plane_size = coeffs.shape
    groups = lax.axis_size("box")
    terms = lax.axis_size("term")
    shape = pltpu.VMEM
    coeffs = coeffs.reshape(degree * box_count, plane_size)
    totals = shape((9, 6 * box_count, plane_size), jnp.float32)
    image = shape((27 * box_count, 2 * plane_size), jnp.bfloat16)

    def swap(value, other):
        return lax.ppermute(value, "term", [(i, other(i) % terms) for i in range(terms)])

    def images(rows, before, final):
        height = 6 * degree * sum(piece.shape[0] for piece in rows)
        count = height // (3 * degree)
        scratch = [
            pltpu.VMEM((height, plane_size), jnp.float32),
            pltpu.VMEM((height, plane_size), jnp.bfloat16),
            pltpu.VMEM((6 * box_count * count, plane_size), jnp.bfloat16),
            pltpu.VMEM((6 * box_count, plane_size * count), jnp.bfloat16),
            pltpu.VMEM((6, plane_size, plane_size * GROUP), jnp.bfloat16),
        ]
        if final:
            scratch.append(pltpu.VMEM((9, 6 * box_count, plane_size), jnp.float32))
        return call(
            functools.partial(image_kernel, count, len(rows), before is None, final),
            (image, image) if final else totals,
            scratch,
            near(coeffs),
            *[near(piece) for piece in rows],
            *([] if before is None else [near(before)]),
        )

    keys, mine, coeffs = call(
        request_kernel,
        (
            shape((groups, 128), jnp.int32),
            shape((1, degree, 128), operators.dtype),
            shape(coeffs.shape, coeffs.dtype),
        ),
        [
            pltpu.VMEM(neighbors.shape, neighbors.dtype),
            pltpu.VMEM((6 * degree, degree), operators.dtype),
            pltpu.SemaphoreType.DMA((3,)),
        ],
        neighbors,
        operators.reshape(-1, degree),
        coeffs,
        place=pl.ANY,
    )
    pieces = [mine]
    for bit in (1, 2, 3):
        pieces.append(swap(mine, functools.partial(lambda bit, i: i ^ bit, bit)))
    guests = lax.all_to_all(keys, "box", split_axis=0, concat_axis=0, tiled=True)
    quad = jnp.concatenate(pieces, axis=0)
    rest = swap(quad, lambda i: i ^ 6)
    total = images([quad], None, False)
    high, low = images([rest], total, True)
    message, local, place = call(
        message_kernel,
        (
            shape((groups, 16, 128), jnp.bfloat16),
            shape((64, 128), jnp.float32),
            shape((64, 16 * groups), jnp.bfloat16),
        ),
        [pltpu.VMEM((groups, 16, 128), jnp.float32)],
        near(keys),
        near(guests),
        near(neighbors),
        near(high),
        near(low),
    )
    ranks = [i ^ flip_of(groups) for i in range(groups)]
    arrived = lax.all_to_all(
        message, "box", split_axis=0, concat_axis=0, tiled=True, axis_index_groups=[ranks]
    )
    return call(
        gather_kernel,
        jax.ShapeDtypeStruct((2, box_count, plane_size), jnp.float32),
        [],
        near(local),
        near(place),
        near(arrived),
    )


def solution(mesh):
    placed = (P(None, "box", None), P("term", None, None, None), P("box", None))
    return jax.shard_map(
        on_device, mesh=mesh, in_specs=placed, out_specs=P("term", "box", None), check_vma=False
    )
```

```python
import functools

import jax
import jax.numpy as jnp
from jax import lax
from jax.experimental import pallas as pl
from jax.experimental.pallas import tpu as pltpu
from jax.sharding import PartitionSpec as P

CAP = 2
GROUP = 4
BIG = 0x7FFFFFFF


def iota(shape, axis):
    return lax.broadcasted_iota(jnp.int32, shape, axis)


def request_kernel(
    neighbors_hbm,
    operators_hbm,
    coeffs_hbm,
    keys_ref,
    own_ref,
    mine_ref,
    near_ref,
    neighbors_ref,
    operators_ref,
    arrivals,
):
    fetches = [
        pltpu.make_async_copy(source, target, arrivals.at[i])
        for i, (source, target) in enumerate(
            (
                (neighbors_hbm, neighbors_ref),
                (operators_hbm, operators_ref),
                (coeffs_hbm, near_ref),
            )
        )
    ]
    for fetch in fetches:
        fetch.start()
    fetches[1].wait()
    blocks = [operators_ref[16 * i : 16 * (i + 1), :] for i in range(6)]
    pad = jnp.zeros((16, 32), operators_ref.dtype)
    mine_ref[0] = jnp.concatenate(blocks + [pad], axis=1)
    fetches[0].wait()
    box_count, column_count = neighbors_ref.shape
    groups = keys_ref.shape[0]
    myself = lax.axis_index("box").astype(jnp.int32)
    peer = iota((groups, column_count), 0)
    column = iota((groups, column_count), 1)
    first = jnp.full((groups, column_count), BIG, jnp.int32)
    last = jnp.full((groups, column_count), -1, jnp.int32)
    for home in range(box_count):
        named = neighbors_ref[home : home + 1, :]
        owner = jnp.where(named >= 0, named >> 4, -1)
        owner = jnp.where(owner == myself, -1, owner)
        key = ((home * column_count + column) << 16) | (column << 8) | (home << 4) | (named & 15)
        member = jnp.broadcast_to(owner, peer.shape) == peer
        first = jnp.minimum(first, jnp.where(member, key, BIG))
        last = jnp.maximum(last, jnp.where(member, key, -1))
    first = jnp.min(first, axis=1, keepdims=True)
    last = jnp.max(last, axis=1, keepdims=True)
    last = jnp.where(last == first, -1, last)
    first = jnp.where(first == BIG, -1, first)
    lane = iota(keys_ref.shape, 1)
    keys = jnp.where(lane == 0, first, jnp.where(lane == 1, last, -1))
    keys_ref[...] = keys
    own_ref[...] = keys
    fetches[2].wait()


def image_kernel(terms, pieces, first, final, coeffs_ref, *refs):
    rows_refs, refs = refs[:pieces], list(refs[pieces:])
    before_ref = None if first else refs.pop(0)
    after_ref = None if final else refs.pop(0)
    high_ref, low_ref = (refs.pop(0), refs.pop(0)) if final else (None, None)
    outer_ref, inner_ref, left_ref, half_ref, kron_ref = refs[:5]
    sum_ref = refs[5] if final else after_ref
    term = lax.axis_index("term").astype(jnp.int32)
    lane = iota((16, 256), 1)
    row = iota((16, 256), 0)
    to_outer = jnp.where((lane >> 4) == row, 1.0, 0.0).astype(jnp.bfloat16)
    to_inner = jnp.where((lane & 15) == row, 1.0, 0.0).astype(jnp.bfloat16)
    blocks = []
    for ref in rows_refs:
        for i in range(ref.shape[0]):
            packed = ref[i]
            blocks += [packed[:, 16 * b : 16 * (b + 1)] for b in range(6)]
    rows = jnp.concatenate(blocks, axis=0)
    outer_ref[...] = jnp.dot(rows, to_outer, preferred_element_type=jnp.float32)
    inner_ref[...] = jnp.dot(rows, to_inner, preferred_element_type=jnp.float32).astype(
        jnp.bfloat16
    )
    diagonal = (lane & 15) == row
    for r in range(terms):
        for m in range(3):
            for al in range(2):
                line = outer_ref[pl.ds(16 * (3 * r + m) + 2 * term + al, 1), :]
                block = jnp.where(diagonal, jnp.broadcast_to(line, (16, 256)), 0.0)
                at = 96 * r + 32 * m + 16 * al
                left_ref[at : at + 16, :] = block.astype(jnp.bfloat16)
    half = jnp.dot(left_ref[...], coeffs_ref[...], preferred_element_type=jnp.float32)
    half = half.astype(jnp.bfloat16)
    for r in range(terms):
        half_ref[:, 256 * r : 256 * (r + 1)] = half[96 * r : 96 * (r + 1), :]
    wide = 256 * GROUP
    for start in range(0, terms, GROUP):
        last = start + GROUP == terms
        for n in range(3):
            slot = 3 * ((3 * (start // GROUP) + n) % 2)
            for r in range(start, start + GROUP):
                to = slice(256 * (r - start), 256 * (r - start + 1))
                inner = [
                    inner_ref[16 * (3 * r + p) : 16 * (3 * r + p + 1), :] for p in range(3)
                ]
                for a in range(16):
                    at = 16 * (3 * r + n) + a
                    line = outer_ref[at : at + 1, :]
                    line = jnp.broadcast_to(line, (16, 256)).astype(jnp.bfloat16)
                    for p in range(3):
                        kron_ref[slot + p, 16 * a : 16 * (a + 1), to] = line * inner[p]
            for p in range(3):
                applied = lax.dot_general(
                    half_ref[:, 256 * start : 256 * start + wide],
                    kron_ref[slot + p],
                    (((1,), (1,)), ((), ())),
                    preferred_element_type=jnp.float32,
                )
                if start:
                    applied = applied + sum_ref[3 * n + p]
                elif not first:
                    applied = applied + before_ref[3 * n + p]
                if not (final and last):
                    sum_ref[3 * n + p] = applied
                    continue
                high = applied.astype(jnp.bfloat16)
                low = (applied - high.astype(jnp.float32)).astype(jnp.bfloat16)
                for m in range(3):
                    code = 9 * m + 3 * n + p
                    for al in range(2):
                        at = 32 * m + 16 * al
                        to = (slice(16 * code, 16 * (code + 1)), slice(256 * al, 256 * (al + 1)))
                        high_ref[to] = high[at : at + 16, :]
                        low_ref[to] = low[at : at + 16, :]


def flip_of(groups):
    return groups // 2 + groups // 8


def flipped(rows):
    groups = rows.shape[0]
    part = groups // 8
    flip = flip_of(groups) // part
    return jnp.concatenate(
        [rows[part * (i ^ flip) : part * ((i ^ flip) + 1), :] for i in range(8)], axis=0
    )


def message_kernel(
    keys_ref,
    guests_ref,
    neighbors_ref,
    high_ref,
    low_ref,
    message_ref,
    local_ref,
    place_ref,
    chunk_ref,
):
    keys = flipped(keys_ref[...])
    guests = flipped(guests_ref[...])
    spots = []
    for slot in range(CAP):
        key = keys[:, slot : slot + 1]
        spot = (12 - ((key >> 8) & 15)) * 16 + ((key >> 4) & 15)
        spots.append(jnp.where(key < 0, -1, spot))
    for slot in range(CAP):
        key = guests[:, slot : slot + 1]
        spot = (14 + ((key >> 8) & 15)) * 16 + (key & 15)
        spots.append(jnp.where(key < 0, -1, spot))
    lane = iota((32, 432), 1)
    picks = jnp.concatenate(
        [jnp.where(lane == spot, 1.0, 0.0).astype(jnp.bfloat16) for spot in spots], axis=0
    )
    picked = jnp.dot(picks, high_ref[...], preferred_element_type=jnp.float32)
    for slot in range(2 * CAP):
        for part in range(4):
            chunk_ref[:, 4 * part + slot, :] = picked[
                32 * slot : 32 * (slot + 1), 128 * part : 128 * (part + 1)
            ]
    message_ref[...] = chunk_ref[...].astype(jnp.bfloat16)
    myself = lax.axis_index("box").astype(jnp.int32)
    named = neighbors_ref[...]
    within = named - 16 * myself
    within = jnp.where((within >= 0) & (within < 16), within, -1).astype(jnp.float32)
    within = within.astype(jnp.bfloat16)
    lane = iota((13, 208), 1)
    row = iota((13, 208), 0)
    ahead = jnp.where((lane >> 4) == row, 1.0, 0.0).astype(jnp.bfloat16)
    behind = jnp.where((lane >> 4) == 12 - row, 1.0, 0.0).astype(jnp.bfloat16)
    pull = jnp.dot(within, ahead, preferred_element_type=jnp.float32).astype(jnp.int32)
    push = jnp.dot(within, behind, preferred_element_type=jnp.float32)
    lane = iota((16, 208), 1) & 15
    row = iota((16, 208), 0)
    push = jnp.sum(jnp.where(lane == row, push, 0.0), axis=0, keepdims=True).astype(jnp.int32)
    pull_mask = jnp.where(pull == lane, 1.0, 0.0)
    push_mask = jnp.where(jnp.broadcast_to(push, row.shape) == row, 1.0, 0.0)
    same_mask = jnp.where(iota((16, 16), 0) == iota((16, 16), 1), 1.0, 0.0)
    mask = jnp.concatenate([push_mask, same_mask, pull_mask], axis=1).astype(jnp.bfloat16)
    local = jnp.dot(mask, high_ref[...], preferred_element_type=jnp.float32) + jnp.dot(
        mask, low_ref[...], preferred_element_type=jnp.float32
    )
    for part in range(4):
        local_ref[16 * part : 16 * (part + 1), :] = local[:, 128 * part : 128 * (part + 1)]
    lane = iota((32, 128), 1)
    keys = jnp.where((lane == 2) | (lane == 3), jnp.roll(keys, 2, axis=1), -1)
    target = jnp.where(lane < 2, guests & 15, (keys >> 4) & 15)
    target = jnp.where(jnp.where(lane < 2, guests, keys) < 0, -1, target)
    spread = jnp.where((iota((32, 512), 1) >> 4) == iota((32, 512), 0), 1.0, 0.0)
    target = lax.dot_general(
        target.astype(jnp.float32).astype(jnp.bfloat16),
        spread.astype(jnp.bfloat16),
        (((0,), (0,)), ((), ())),
        preferred_element_type=jnp.float32,
    )[:8]
    lane = iota((8, 512), 1)
    target = jnp.sum(
        jnp.where((lane & 3) == iota((8, 512), 0), target, 0.0), axis=0, keepdims=True
    ).astype(jnp.int32)
    lane = iota((64, 512), 1)
    row = iota((64, 512), 0)
    place = (jnp.broadcast_to(target, lane.shape) == (row & 15)) & (((lane >> 2) & 3) == (row >> 4))
    place_ref[...] = jnp.where(place, 1.0, 0.0).astype(jnp.bfloat16)


def gather_kernel(local_ref, place_ref, arrived_ref, out_ref):
    total = local_ref[...] + jnp.dot(
        place_ref[...], arrived_ref[...].reshape(512, 128), preferred_element_type=jnp.float32
    )
    for part in range(4):
        out_ref[part // 2, :, 128 * (part % 2) : 128 * (part % 2 + 1)] = total[
            16 * part : 16 * (part + 1), :
        ]


def call(kernel, outs, scratch, *args, place=pltpu.VMEM):
    vmem = pl.BlockSpec(memory_space=pltpu.VMEM)
    return pl.pallas_call(
        kernel,
        out_shape=outs,
        in_specs=[pl.BlockSpec(memory_space=place)] * len(args),
        out_specs=jax.tree.map(lambda _: vmem, outs),
        scratch_shapes=scratch,
    )(*args)


def near(value):
    return pltpu.with_memory_space_constraint(value, pltpu.VMEM)


def on_device(coeffs, operators, neighbors):
    degree, box_count, plane_size = coeffs.shape
    groups = lax.axis_size("box")
    terms = lax.axis_size("term")
    shape = pltpu.VMEM
    coeffs = coeffs.reshape(degree * box_count, plane_size)
    totals = shape((9, 6 * box_count, plane_size), jnp.float32)
    image = shape((27 * box_count, 2 * plane_size), jnp.bfloat16)

    def swap(value, other):
        return lax.ppermute(value, "term", [(i, other(i) % terms) for i in range(terms)])

    def images(rows, before, final):
        height = 6 * degree * sum(piece.shape[0] for piece in rows)
        count = height // (3 * degree)
        scratch = [
            pltpu.VMEM((height, plane_size), jnp.float32),
            pltpu.VMEM((height, plane_size), jnp.bfloat16),
            pltpu.VMEM((6 * box_count * count, plane_size), jnp.bfloat16),
            pltpu.VMEM((6 * box_count, plane_size * count), jnp.bfloat16),
            pltpu.VMEM((6, plane_size, plane_size * GROUP), jnp.bfloat16),
        ]
        if final:
            scratch.append(pltpu.VMEM((9, 6 * box_count, plane_size), jnp.float32))
        return call(
            functools.partial(image_kernel, count, len(rows), before is None, final),
            (image, image) if final else totals,
            scratch,
            near(coeffs),
            *[near(piece) for piece in rows],
            *([] if before is None else [near(before)]),
        )

    keys, own, mine, coeffs = call(
        request_kernel,
        (
            shape((groups, 128), jnp.int32),
            shape((groups, 128), jnp.int32),
            shape((1, degree, 128), operators.dtype),
            shape(coeffs.shape, coeffs.dtype),
        ),
        [
            pltpu.VMEM(neighbors.shape, neighbors.dtype),
            pltpu.VMEM((6 * degree, degree), operators.dtype),
            pltpu.SemaphoreType.DMA((3,)),
        ],
        neighbors,
        operators.reshape(-1, degree),
        coeffs,
        place=pl.ANY,
    )
    pieces = [mine]
    for bit in (1, 2, 3):
        pieces.append(swap(mine, functools.partial(lambda bit, i: i ^ bit, bit)))
    guests = lax.all_to_all(keys, "box", split_axis=0, concat_axis=0, tiled=True)
    quad = jnp.concatenate(pieces, axis=0)
    rest = swap(quad, lambda i: i ^ 6)
    total = images([quad], None, False)
    high, low = images([rest], total, True)
    message, local, place = call(
        message_kernel,
        (
            shape((groups, 16, 128), jnp.bfloat16),
            shape((64, 128), jnp.float32),
            shape((64, 16 * groups), jnp.bfloat16),
        ),
        [pltpu.VMEM((groups, 16, 128), jnp.float32)],
        near(own),
        near(guests),
        near(neighbors),
        near(high),
        near(low),
    )
    ranks = [i ^ flip_of(groups) for i in range(groups)]
    arrived = lax.all_to_all(
        message, "box", split_axis=0, concat_axis=0, tiled=True, axis_index_groups=[ranks]
    )
    return call(
        gather_kernel,
        jax.ShapeDtypeStruct((2, box_count, plane_size), jnp.float32),
        [],
        near(local),
        near(place),
        near(arrived),
    )


def solution(mesh):
    placed = (P(None, "box", None), P("term", None, None, None), P("box", None))
    return jax.shard_map(
        on_device, mesh=mesh, in_specs=placed, out_specs=P("term", "box", None), check_vma=False
    )
```

```python
import functools

import jax
import jax.numpy as jnp
from jax import lax
from jax.experimental import pallas as pl
from jax.experimental.pallas import tpu as pltpu
from jax.sharding import PartitionSpec as P

CAP = 2
BIG = 0x7FFFFFFF


def iota(shape, axis):
    return lax.broadcasted_iota(jnp.int32, shape, axis)


def request_kernel(
    neighbors_hbm,
    operators_hbm,
    coeffs_hbm,
    keys_ref,
    own_ref,
    mine_ref,
    near_ref,
    neighbors_ref,
    operators_ref,
    arrivals,
):
    fetches = [
        pltpu.make_async_copy(source, target, arrivals.at[i])
        for i, (source, target) in enumerate(
            (
                (neighbors_hbm, neighbors_ref),
                (operators_hbm, operators_ref),
                (coeffs_hbm, near_ref),
            )
        )
    ]
    for fetch in fetches:
        fetch.start()
    fetches[1].wait()
    blocks = [operators_ref[16 * i : 16 * (i + 1), :] for i in range(6)]
    pad = jnp.zeros((16, 32), operators_ref.dtype)
    mine_ref[0] = jnp.concatenate(blocks + [pad], axis=1)
    fetches[0].wait()
    box_count, column_count = neighbors_ref.shape
    groups = keys_ref.shape[0]
    myself = lax.axis_index("box").astype(jnp.int32)
    peer = iota((groups, column_count), 0)
    column = iota((groups, column_count), 1)
    first = jnp.full((groups, column_count), BIG, jnp.int32)
    last = jnp.full((groups, column_count), -1, jnp.int32)
    for home in range(box_count):
        named = neighbors_ref[home : home + 1, :]
        owner = jnp.where(named >= 0, named >> 4, -1)
        owner = jnp.where(owner == myself, -1, owner)
        key = ((home * column_count + column) << 16) | (column << 8) | (home << 4) | (named & 15)
        member = jnp.broadcast_to(owner, peer.shape) == peer
        first = jnp.minimum(first, jnp.where(member, key, BIG))
        last = jnp.maximum(last, jnp.where(member, key, -1))
    first = jnp.min(first, axis=1, keepdims=True)
    last = jnp.max(last, axis=1, keepdims=True)
    last = jnp.where(last == first, -1, last)
    first = jnp.where(first == BIG, -1, first)
    lane = iota(keys_ref.shape, 1)
    keys = jnp.where(lane == 0, first, jnp.where(lane == 1, last, -1))
    keys_ref[...] = keys
    own_ref[...] = keys
    fetches[2].wait()


def image_kernel(terms, pieces, first, final, coeffs_ref, *refs):
    rows_refs, refs = refs[:pieces], list(refs[pieces:])
    before_ref = None if first else refs.pop(0)
    after_ref = None if final else refs.pop(0)
    high_ref, low_ref = (refs.pop(0), refs.pop(0)) if final else (None, None)
    outer_ref, inner_ref, left_ref, half_ref, along_ref, across_ref = refs
    term = lax.axis_index("term").astype(jnp.int32)
    lane = iota((16, 256), 1)
    row = iota((16, 256), 0)
    to_outer = jnp.where((lane >> 4) == row, 1.0, 0.0).astype(jnp.bfloat16)
    equal = (lane & 15) == row
    to_inner = jnp.where(equal, 1.0, 0.0).astype(jnp.bfloat16)
    blocks = []
    for ref in rows_refs:
        for i in range(ref.shape[0]):
            packed = ref[i]
            blocks += [packed[:, 16 * b : 16 * (b + 1)] for b in range(6)]
    rows = jnp.concatenate(blocks, axis=0)
    outer_ref[...] = jnp.dot(rows, to_outer, preferred_element_type=jnp.float32)
    inner_ref[...] = jnp.dot(
        rows, to_inner[:, :128], preferred_element_type=jnp.float32
    ).astype(jnp.bfloat16)
    for r in range(terms):
        for m in range(3):
            for al in range(2):
                line = outer_ref[pl.ds(16 * (3 * r + m) + 2 * term + al, 1), :]
                block = jnp.where(equal, jnp.broadcast_to(line, (16, 256)), 0.0)
                at = 96 * r + 32 * m + 16 * al
                left_ref[at : at + 16, :] = block.astype(jnp.bfloat16)
    half = jnp.dot(left_ref[...], coeffs_ref[...], preferred_element_type=jnp.float32)
    half = half.astype(jnp.bfloat16)
    for r in range(terms):
        for side in range(2):
            half_ref[r, 96 * side : 96 * (side + 1), :] = half[
                96 * r : 96 * (r + 1), 128 * side : 128 * (side + 1)
            ]
    lane = iota((16, 128), 1)
    keep = [jnp.where((lane >> 4) == c, 1.0, 0.0).astype(jnp.bfloat16) for c in range(8)]
    for r in range(terms):
        matrix = jnp.concatenate(
            [
                inner_ref[16 * (3 * r + p) : 16 * (3 * r + p + 1), :] * keep[c]
                for p in range(3)
                for c in range(8)
            ],
            axis=0,
        )
        applied = lax.dot_general(
            half_ref[r], matrix, (((1,), (1,)), ((), ())), preferred_element_type=jnp.float32
        ).astype(jnp.bfloat16)
        for p in range(3):
            for side in range(2):
                at = 256 * r + 128 * side
                along_ref[96 * p : 96 * (p + 1), at : at + 128] = applied[
                    96 * side : 96 * (side + 1), 128 * p : 128 * (p + 1)
                ]
    for n in range(3):
        for r in range(terms):
            for a in range(16):
                at = 16 * (3 * r + n) + a
                line = outer_ref[at : at + 1, :]
                line = jnp.broadcast_to(line, (16, 256)).astype(jnp.bfloat16)
                across_ref[n, 16 * a : 16 * (a + 1), 256 * r : 256 * (r + 1)] = line * to_inner
        applied = lax.dot_general(
            along_ref[...],
            across_ref[n],
            (((1,), (1,)), ((), ())),
            preferred_element_type=jnp.float32,
        )
        if not first:
            applied = applied + before_ref[n]
        if not final:
            after_ref[n] = applied
            continue
        high = applied.astype(jnp.bfloat16)
        low = (applied - high.astype(jnp.float32)).astype(jnp.bfloat16)
        for p in range(3):
            for m in range(3):
                code = 9 * m + 3 * n + p
                for al in range(2):
                    at = 96 * p + 32 * m + 16 * al
                    to = (slice(16 * code, 16 * (code + 1)), slice(256 * al, 256 * (al + 1)))
                    high_ref[to] = high[at : at + 16, :]
                    low_ref[to] = low[at : at + 16, :]


def flip_of(groups):
    return groups // 2 + groups // 8


def flipped(rows):
    groups = rows.shape[0]
    part = groups // 8
    flip = flip_of(groups) // part
    return jnp.concatenate(
        [rows[part * (i ^ flip) : part * ((i ^ flip) + 1), :] for i in range(8)], axis=0
    )


def message_kernel(
    keys_ref,
    guests_ref,
    neighbors_ref,
    high_ref,
    low_ref,
    message_ref,
    local_ref,
    place_ref,
    chunk_ref,
):
    keys = flipped(keys_ref[...])
    guests = flipped(guests_ref[...])
    spots = []
    for slot in range(CAP):
        key = keys[:, slot : slot + 1]
        spot = (12 - ((key >> 8) & 15)) * 16 + ((key >> 4) & 15)
        spots.append(jnp.where(key < 0, -1, spot))
    for slot in range(CAP):
        key = guests[:, slot : slot + 1]
        spot = (14 + ((key >> 8) & 15)) * 16 + (key & 15)
        spots.append(jnp.where(key < 0, -1, spot))
    lane = iota((32, 432), 1)
    picks = jnp.concatenate(
        [jnp.where(lane == spot, 1.0, 0.0).astype(jnp.bfloat16) for spot in spots], axis=0
    )
    picked = jnp.dot(picks, high_ref[...], preferred_element_type=jnp.float32)
    for slot in range(2 * CAP):
        for part in range(4):
            chunk_ref[:, 4 * part + slot, :] = picked[
                32 * slot : 32 * (slot + 1), 128 * part : 128 * (part + 1)
            ]
    message_ref[...] = chunk_ref[...].astype(jnp.bfloat16)
    myself = lax.axis_index("box").astype(jnp.int32)
    named = neighbors_ref[...]
    within = named - 16 * myself
    within = jnp.where((within >= 0) & (within < 16), within, -1).astype(jnp.float32)
    within = within.astype(jnp.bfloat16)
    lane = iota((13, 208), 1)
    row = iota((13, 208), 0)
    ahead = jnp.where((lane >> 4) == row, 1.0, 0.0).astype(jnp.bfloat16)
    behind = jnp.where((lane >> 4) == 12 - row, 1.0, 0.0).astype(jnp.bfloat16)
    pull = jnp.dot(within, ahead, preferred_element_type=jnp.float32).astype(jnp.int32)
    push = jnp.dot(within, behind, preferred_element_type=jnp.float32)
    lane = iota((16, 208), 1) & 15
    row = iota((16, 208), 0)
    push = jnp.sum(jnp.where(lane == row, push, 0.0), axis=0, keepdims=True).astype(jnp.int32)
    pull_mask = jnp.where(pull == lane, 1.0, 0.0)
    push_mask = jnp.where(jnp.broadcast_to(push, row.shape) == row, 1.0, 0.0)
    same_mask = jnp.where(iota((16, 16), 0) == iota((16, 16), 1), 1.0, 0.0)
    mask = jnp.concatenate([push_mask, same_mask, pull_mask], axis=1).astype(jnp.bfloat16)
    local = jnp.dot(mask, high_ref[...], preferred_element_type=jnp.float32) + jnp.dot(
        mask, low_ref[...], preferred_element_type=jnp.float32
    )
    for part in range(4):
        local_ref[16 * part : 16 * (part + 1), :] = local[:, 128 * part : 128 * (part + 1)]
    lane = iota((32, 128), 1)
    keys = jnp.where((lane == 2) | (lane == 3), jnp.roll(keys, 2, axis=1), -1)
    target = jnp.where(lane < 2, guests & 15, (keys >> 4) & 15)
    target = jnp.where(jnp.where(lane < 2, guests, keys) < 0, -1, target)
    spread = jnp.where((iota((32, 512), 1) >> 4) == iota((32, 512), 0), 1.0, 0.0)
    target = lax.dot_general(
        target.astype(jnp.float32).astype(jnp.bfloat16),
        spread.astype(jnp.bfloat16),
        (((0,), (0,)), ((), ())),
        preferred_element_type=jnp.float32,
    )[:8]
    lane = iota((8, 512), 1)
    target = jnp.sum(
        jnp.where((lane & 3) == iota((8, 512), 0), target, 0.0), axis=0, keepdims=True
    ).astype(jnp.int32)
    lane = iota((64, 512), 1)
    row = iota((64, 512), 0)
    place = (jnp.broadcast_to(target, lane.shape) == (row & 15)) & (((lane >> 2) & 3) == (row >> 4))
    place_ref[...] = jnp.where(place, 1.0, 0.0).astype(jnp.bfloat16)


def gather_kernel(local_ref, place_ref, arrived_ref, out_ref):
    total = local_ref[...] + jnp.dot(
        place_ref[...], arrived_ref[...].reshape(512, 128), preferred_element_type=jnp.float32
    )
    for part in range(4):
        out_ref[part // 2, :, 128 * (part % 2) : 128 * (part % 2 + 1)] = total[
            16 * part : 16 * (part + 1), :
        ]


def call(kernel, outs, scratch, *args, place=pltpu.VMEM):
    vmem = pl.BlockSpec(memory_space=pltpu.VMEM)
    return pl.pallas_call(
        kernel,
        out_shape=outs,
        in_specs=[pl.BlockSpec(memory_space=place)] * len(args),
        out_specs=jax.tree.map(lambda _: vmem, outs),
        scratch_shapes=scratch,
    )(*args)


def near(value):
    return pltpu.with_memory_space_constraint(value, pltpu.VMEM)


def on_device(coeffs, operators, neighbors):
    degree, box_count, plane_size = coeffs.shape
    groups = lax.axis_size("box")
    terms = lax.axis_size("term")
    shape = pltpu.VMEM
    coeffs = coeffs.reshape(degree * box_count, plane_size)
    totals = shape((3, 18 * box_count, plane_size), jnp.float32)
    image = shape((27 * box_count, 2 * plane_size), jnp.bfloat16)

    def swap(value, other):
        return lax.ppermute(value, "term", [(i, other(i) % terms) for i in range(terms)])

    def images(rows, before, final):
        height = 6 * degree * sum(piece.shape[0] for piece in rows)
        count = height // (3 * degree)
        scratch = [
            pltpu.VMEM((height, plane_size), jnp.float32),
            pltpu.VMEM((height, plane_size // 2), jnp.bfloat16),
            pltpu.VMEM((6 * box_count * count, plane_size), jnp.bfloat16),
            pltpu.VMEM((count, 12 * box_count, plane_size // 2), jnp.bfloat16),
            pltpu.VMEM((18 * box_count, plane_size * count), jnp.bfloat16),
            pltpu.VMEM((3, plane_size, plane_size * count), jnp.bfloat16),
        ]
        return call(
            functools.partial(image_kernel, count, len(rows), before is None, final),
            (image, image) if final else totals,
            scratch,
            near(coeffs),
            *[near(piece) for piece in rows],
            *([] if before is None else [near(before)]),
        )

    keys, own, mine, coeffs = call(
        request_kernel,
        (
            shape((groups, 128), jnp.int32),
            shape((groups, 128), jnp.int32),
            shape((1, degree, 128), operators.dtype),
            shape(coeffs.shape, coeffs.dtype),
        ),
        [
            pltpu.VMEM(neighbors.shape, neighbors.dtype),
            pltpu.VMEM((6 * degree, degree), operators.dtype),
            pltpu.SemaphoreType.DMA((3,)),
        ],
        neighbors,
        operators.reshape(-1, degree),
        coeffs,
        place=pl.ANY,
    )
    pieces = [mine]
    for bit in (1, 2, 3):
        pieces.append(swap(mine, functools.partial(lambda bit, i: i ^ bit, bit)))
    guests = lax.all_to_all(keys, "box", split_axis=0, concat_axis=0, tiled=True)
    quad = jnp.concatenate(pieces, axis=0)
    rest = swap(quad, lambda i: i ^ 6)
    total = images([quad], None, False)
    high, low = images([rest], total, True)
    message, local, place = call(
        message_kernel,
        (
            shape((groups, 16, 128), jnp.bfloat16),
            shape((64, 128), jnp.float32),
            shape((64, 16 * groups), jnp.bfloat16),
        ),
        [pltpu.VMEM((groups, 16, 128), jnp.float32)],
        near(own),
        near(guests),
        near(neighbors),
        near(high),
        near(low),
    )
    ranks = [i ^ flip_of(groups) for i in range(groups)]
    arrived = lax.all_to_all(
        message, "box", split_axis=0, concat_axis=0, tiled=True, axis_index_groups=[ranks]
    )
    return call(
        gather_kernel,
        jax.ShapeDtypeStruct((2, box_count, plane_size), jnp.float32),
        [],
        near(local),
        near(place),
        near(arrived),
    )


def solution(mesh):
    placed = (P(None, "box", None), P("term", None, None, None), P("box", None))
    return jax.shard_map(
        on_device, mesh=mesh, in_specs=placed, out_specs=P("term", "box", None), check_vma=False
    )
```

```python
import functools

import jax
import jax.numpy as jnp
from jax import lax
from jax.experimental import pallas as pl
from jax.experimental.pallas import tpu as pltpu
from jax.sharding import PartitionSpec as P

CAP = 2
BIG = 0x7FFFFFFF


def iota(shape, axis):
    return lax.broadcasted_iota(jnp.int32, shape, axis)


def request_kernel(
    neighbors_hbm,
    operators_hbm,
    coeffs_hbm,
    keys_ref,
    own_ref,
    mine_ref,
    near_ref,
    neighbors_ref,
    operators_ref,
    arrivals,
):
    fetches = [
        pltpu.make_async_copy(source, target, arrivals.at[i])
        for i, (source, target) in enumerate(
            (
                (neighbors_hbm, neighbors_ref),
                (operators_hbm, operators_ref),
                (coeffs_hbm, near_ref),
            )
        )
    ]
    for fetch in fetches:
        fetch.start()
    fetches[1].wait()
    blocks = [operators_ref[16 * i : 16 * (i + 1), :] for i in range(6)]
    pad = jnp.zeros((16, 32), operators_ref.dtype)
    mine_ref[0] = jnp.concatenate(blocks + [pad], axis=1)
    fetches[0].wait()
    box_count, column_count = neighbors_ref.shape
    groups = keys_ref.shape[0]
    myself = lax.axis_index("box").astype(jnp.int32)
    peer = iota((groups, column_count), 0)
    column = iota((groups, column_count), 1)
    first = jnp.full((groups, column_count), BIG, jnp.int32)
    last = jnp.full((groups, column_count), -1, jnp.int32)
    for home in range(box_count):
        named = neighbors_ref[home : home + 1, :]
        owner = jnp.where(named >= 0, named >> 4, -1)
        owner = jnp.where(owner == myself, -1, owner)
        key = ((home * column_count + column) << 16) | (column << 8) | (home << 4) | (named & 15)
        member = jnp.broadcast_to(owner, peer.shape) == peer
        first = jnp.minimum(first, jnp.where(member, key, BIG))
        last = jnp.maximum(last, jnp.where(member, key, -1))
    first = jnp.min(first, axis=1, keepdims=True)
    last = jnp.max(last, axis=1, keepdims=True)
    last = jnp.where(last == first, -1, last)
    first = jnp.where(first == BIG, -1, first)
    lane = iota(keys_ref.shape, 1)
    keys = jnp.where(lane == 0, first, jnp.where(lane == 1, last, -1))
    keys_ref[...] = keys
    own_ref[...] = keys
    fetches[2].wait()


def image_kernel(terms, pieces, first, final, coeffs_ref, *refs):
    rows_refs, refs = refs[:pieces], list(refs[pieces:])
    before_ref = None if first else refs.pop(0)
    after_ref = None if final else refs.pop(0)
    high_ref, low_ref = (refs.pop(0), refs.pop(0)) if final else (None, None)
    outer_ref, inner_ref, left_ref, half_ref, along_ref, across_ref = refs
    term = lax.axis_index("term").astype(jnp.int32)
    lane = iota((16, 256), 1)
    row = iota((16, 256), 0)
    to_outer = jnp.where((lane >> 4) == row, 1.0, 0.0).astype(jnp.bfloat16)
    equal = (lane & 15) == row
    to_inner = jnp.where(equal, 1.0, 0.0).astype(jnp.bfloat16)
    blocks = []
    for ref in rows_refs:
        for i in range(ref.shape[0]):
            packed = ref[i]
            blocks += [packed[:, 16 * b : 16 * (b + 1)] for b in range(6)]
    rows = jnp.concatenate(blocks, axis=0)
    outer_ref[...] = jnp.dot(rows, to_outer, preferred_element_type=jnp.float32)
    inner_ref[...] = jnp.dot(
        rows, to_inner[:, :128], preferred_element_type=jnp.float32
    ).astype(jnp.bfloat16)
    for r in range(terms):
        for m in range(3):
            for al in range(2):
                line = outer_ref[pl.ds(16 * (3 * r + m) + 2 * term + al, 1), :]
                block = jnp.where(equal, jnp.broadcast_to(line, (16, 256)), 0.0)
                at = 96 * r + 32 * m + 16 * al
                left_ref[at : at + 16, :] = block.astype(jnp.bfloat16)
    half = jnp.dot(left_ref[...], coeffs_ref[...], preferred_element_type=jnp.float32)
    half = half.astype(jnp.bfloat16)
    for r in range(terms):
        for side in range(2):
            half_ref[r, 96 * side : 96 * (side + 1), :] = half[
                96 * r : 96 * (r + 1), 128 * side : 128 * (side + 1)
            ]
    lane = iota((16, 128), 1)
    keep = [jnp.where((lane >> 4) == c, 1.0, 0.0).astype(jnp.bfloat16) for c in range(8)]
    for r in range(terms):
        matrix = jnp.concatenate(
            [
                inner_ref[16 * (3 * r + p) : 16 * (3 * r + p + 1), :] * keep[c]
                for p in range(3)
                for c in range(8)
            ],
            axis=0,
        )
        applied = lax.dot_general(
            half_ref[r], matrix, (((1,), (1,)), ((), ())), preferred_element_type=jnp.float32
        ).astype(jnp.bfloat16)
        for p in range(3):
            for side in range(2):
                at = 256 * r + 128 * side
                along_ref[96 * p : 96 * (p + 1), at : at + 128] = applied[
                    96 * side : 96 * (side + 1), 128 * p : 128 * (p + 1)
                ]
    for n in range(3):
        for r in range(terms):
            for a in range(16):
                at = 16 * (3 * r + n) + a
                line = outer_ref[at : at + 1, :]
                line = jnp.broadcast_to(line, (16, 256)).astype(jnp.bfloat16)
                across_ref[n, 16 * a : 16 * (a + 1), 256 * r : 256 * (r + 1)] = line * to_inner
        applied = lax.dot_general(
            along_ref[...],
            across_ref[n],
            (((1,), (1,)), ((), ())),
            preferred_element_type=jnp.float32,
        )
        if not first:
            applied = applied + before_ref[n]
        if not final:
            after_ref[n] = applied
            continue
        high = applied.astype(jnp.bfloat16)
        low = (applied - high.astype(jnp.float32)).astype(jnp.bfloat16)
        for p in range(3):
            for m in range(3):
                code = 9 * m + 3 * n + p
                for al in range(2):
                    at = 96 * p + 32 * m + 16 * al
                    to = (slice(16 * code, 16 * (code + 1)), slice(256 * al, 256 * (al + 1)))
                    high_ref[to] = high[at : at + 16, :]
                    low_ref[to] = low[at : at + 16, :]


def flip_of(groups):
    return groups // 2 + groups // 8


def flipped(rows):
    groups = rows.shape[0]
    part = groups // 8
    flip = flip_of(groups) // part
    return jnp.concatenate(
        [rows[part * (i ^ flip) : part * ((i ^ flip) + 1), :] for i in range(8)], axis=0
    )


def select_kernel(keys_ref, guests_ref, neighbors_ref, picks_ref, mask_ref, place_ref):
    keys = flipped(keys_ref[...])
    guests = flipped(guests_ref[...])
    spots = []
    for slot in range(CAP):
        key = keys[:, slot : slot + 1]
        spot = (12 - ((key >> 8) & 15)) * 16 + ((key >> 4) & 15)
        spots.append(jnp.where(key < 0, -1, spot))
    for slot in range(CAP):
        key = guests[:, slot : slot + 1]
        spot = (14 + ((key >> 8) & 15)) * 16 + (key & 15)
        spots.append(jnp.where(key < 0, -1, spot))
    lane = iota((32, 432), 1)
    picks = jnp.concatenate(
        [jnp.where(lane == spot, 1.0, 0.0).astype(jnp.bfloat16) for spot in spots], axis=0
    )
    picks_ref[...] = picks
    myself = lax.axis_index("box").astype(jnp.int32)
    named = neighbors_ref[...]
    within = named - 16 * myself
    within = jnp.where((within >= 0) & (within < 16), within, -1).astype(jnp.float32)
    within = within.astype(jnp.bfloat16)
    lane = iota((13, 208), 1)
    row = iota((13, 208), 0)
    ahead = jnp.where((lane >> 4) == row, 1.0, 0.0).astype(jnp.bfloat16)
    behind = jnp.where((lane >> 4) == 12 - row, 1.0, 0.0).astype(jnp.bfloat16)
    pull = jnp.dot(within, ahead, preferred_element_type=jnp.float32).astype(jnp.int32)
    push = jnp.dot(within, behind, preferred_element_type=jnp.float32)
    lane = iota((16, 208), 1) & 15
    row = iota((16, 208), 0)
    push = jnp.sum(jnp.where(lane == row, push, 0.0), axis=0, keepdims=True).astype(jnp.int32)
    pull_mask = jnp.where(pull == lane, 1.0, 0.0)
    push_mask = jnp.where(jnp.broadcast_to(push, row.shape) == row, 1.0, 0.0)
    same_mask = jnp.where(iota((16, 16), 0) == iota((16, 16), 1), 1.0, 0.0)
    mask = jnp.concatenate([push_mask, same_mask, pull_mask], axis=1).astype(jnp.bfloat16)
    mask_ref[...] = mask
    lane = iota((32, 128), 1)
    keys = jnp.where((lane == 2) | (lane == 3), jnp.roll(keys, 2, axis=1), -1)
    target = jnp.where(lane < 2, guests & 15, (keys >> 4) & 15)
    target = jnp.where(jnp.where(lane < 2, guests, keys) < 0, -1, target)
    spread = jnp.where((iota((32, 512), 1) >> 4) == iota((32, 512), 0), 1.0, 0.0)
    target = lax.dot_general(
        target.astype(jnp.float32).astype(jnp.bfloat16),
        spread.astype(jnp.bfloat16),
        (((0,), (0,)), ((), ())),
        preferred_element_type=jnp.float32,
    )[:8]
    lane = iota((8, 512), 1)
    target = jnp.sum(
        jnp.where((lane & 3) == iota((8, 512), 0), target, 0.0), axis=0, keepdims=True
    ).astype(jnp.int32)
    lane = iota((64, 512), 1)
    row = iota((64, 512), 0)
    place = (jnp.broadcast_to(target, lane.shape) == (row & 15)) & (((lane >> 2) & 3) == (row >> 4))
    place_ref[...] = jnp.where(place, 1.0, 0.0).astype(jnp.bfloat16)


def message_kernel(picks_ref, mask_ref, high_ref, low_ref, message_ref, local_ref, chunk_ref):
    picked = jnp.dot(picks_ref[...], high_ref[...], preferred_element_type=jnp.float32)
    for slot in range(2 * CAP):
        for part in range(4):
            chunk_ref[:, 4 * part + slot, :] = picked[
                32 * slot : 32 * (slot + 1), 128 * part : 128 * (part + 1)
            ]
    message_ref[...] = chunk_ref[...].astype(jnp.bfloat16)
    mask = mask_ref[...]
    local = jnp.dot(mask, high_ref[...], preferred_element_type=jnp.float32) + jnp.dot(
        mask, low_ref[...], preferred_element_type=jnp.float32
    )
    for part in range(4):
        local_ref[16 * part : 16 * (part + 1), :] = local[:, 128 * part : 128 * (part + 1)]


def gather_kernel(local_ref, place_ref, arrived_ref, out_ref):
    total = local_ref[...] + jnp.dot(
        place_ref[...], arrived_ref[...].reshape(512, 128), preferred_element_type=jnp.float32
    )
    for part in range(4):
        out_ref[part // 2, :, 128 * (part % 2) : 128 * (part % 2 + 1)] = total[
            16 * part : 16 * (part + 1), :
        ]


def call(kernel, outs, scratch, *args, place=pltpu.VMEM):
    vmem = pl.BlockSpec(memory_space=pltpu.VMEM)
    return pl.pallas_call(
        kernel,
        out_shape=outs,
        in_specs=[pl.BlockSpec(memory_space=place)] * len(args),
        out_specs=jax.tree.map(lambda _: vmem, outs),
        scratch_shapes=scratch,
    )(*args)


def near(value):
    return pltpu.with_memory_space_constraint(value, pltpu.VMEM)


def on_device(coeffs, operators, neighbors):
    degree, box_count, plane_size = coeffs.shape
    groups = lax.axis_size("box")
    terms = lax.axis_size("term")
    shape = pltpu.VMEM
    coeffs = coeffs.reshape(degree * box_count, plane_size)
    totals = shape((3, 18 * box_count, plane_size), jnp.float32)
    image = shape((27 * box_count, 2 * plane_size), jnp.bfloat16)

    def swap(value, other):
        return lax.ppermute(value, "term", [(i, other(i) % terms) for i in range(terms)])

    def images(rows, before, final):
        height = 6 * degree * sum(piece.shape[0] for piece in rows)
        count = height // (3 * degree)
        scratch = [
            pltpu.VMEM((height, plane_size), jnp.float32),
            pltpu.VMEM((height, plane_size // 2), jnp.bfloat16),
            pltpu.VMEM((6 * box_count * count, plane_size), jnp.bfloat16),
            pltpu.VMEM((count, 12 * box_count, plane_size // 2), jnp.bfloat16),
            pltpu.VMEM((18 * box_count, plane_size * count), jnp.bfloat16),
            pltpu.VMEM((3, plane_size, plane_size * count), jnp.bfloat16),
        ]
        return call(
            functools.partial(image_kernel, count, len(rows), before is None, final),
            (image, image) if final else totals,
            scratch,
            near(coeffs),
            *[near(piece) for piece in rows],
            *([] if before is None else [near(before)]),
        )

    keys, own, mine, coeffs = call(
        request_kernel,
        (
            shape((groups, 128), jnp.int32),
            shape((groups, 128), jnp.int32),
            shape((1, degree, 128), operators.dtype),
            shape(coeffs.shape, coeffs.dtype),
        ),
        [
            pltpu.VMEM(neighbors.shape, neighbors.dtype),
            pltpu.VMEM((6 * degree, degree), operators.dtype),
            pltpu.SemaphoreType.DMA((3,)),
        ],
        neighbors,
        operators.reshape(-1, degree),
        coeffs,
        place=pl.ANY,
    )
    pieces = [mine]
    for bit in (1, 2, 3):
        pieces.append(swap(mine, functools.partial(lambda bit, i: i ^ bit, bit)))
    guests = lax.all_to_all(keys, "box", split_axis=0, concat_axis=0, tiled=True)
    quad = jnp.concatenate(pieces, axis=0)
    rest = swap(quad, lambda i: i ^ 6)
    total = images([quad], None, False)
    picks, mask, place = call(
        select_kernel,
        (
            shape((2 * CAP * groups, 27 * box_count), jnp.bfloat16),
            shape((box_count, 27 * box_count), jnp.bfloat16),
            shape((64, 16 * groups), jnp.bfloat16),
        ),
        [],
        near(own),
        near(guests),
        near(neighbors),
    )
    high, low = images([rest], total, True)
    message, local = call(
        message_kernel,
        (shape((groups, 16, 128), jnp.bfloat16), shape((64, 128), jnp.float32)),
        [pltpu.VMEM((groups, 16, 128), jnp.float32)],
        near(picks),
        near(mask),
        near(high),
        near(low),
    )
    ranks = [i ^ flip_of(groups) for i in range(groups)]
    arrived = lax.all_to_all(
        message, "box", split_axis=0, concat_axis=0, tiled=True, axis_index_groups=[ranks]
    )
    return call(
        gather_kernel,
        jax.ShapeDtypeStruct((2, box_count, plane_size), jnp.float32),
        [],
        near(local),
        near(place),
        near(arrived),
    )


def solution(mesh):
    placed = (P(None, "box", None), P("term", None, None, None), P("box", None))
    return jax.shard_map(
        on_device, mesh=mesh, in_specs=placed, out_specs=P("term", "box", None), check_vma=False
    )
```
